256 devices in a mesh: orbit: 16 (over y_hi, z), space: 16 (over x, y_lo, core).
Axes of the slice: x: 4, y: 4 (y_hi: 2, y_lo: 2; y = y_hi * 2 + y_lo), z: 8, core: 2. Of those that a mesh axis runs over, the one named last changes fastest.
Arguments:
- latents: bfloat16 [64, 16, 16, 1024], P('orbit', 'space'), may hold values from -6 to 6
- conv_gain: float32 [1024], replicated, may hold values from 0.1 to 1.9
- spatial_weight: bfloat16 [3, 3, 1024, 1024], P(None, None, 'space'), may hold values from -0.0625 to 0.0625
- temporal_weight: bfloat16 [3, 1024, 1024], P(None, 'space'), may hold values from -0.109375 to 0.109375
- attn_gain: float32 [1024], replicated, may hold values from 0.1 to 1.9
- qkv_weight: bfloat16 [3, 1024, 1024], P(None, 'space'), may hold values from -0.1875 to 0.1875
- out_weight: bfloat16 [1024, 1024], P('space'), may hold values from -0.1875 to 0.1875
Outputs:
- restored: bfloat16 [64, 16, 16, 1024], P('orbit', 'space')
The draws below stay inside these ranges and needn't reach their ends.
All inputs are finite; a program needn't handle non-finite values.
Results may differ from the reference program's by a relative error of at most 0.029.
Values may be sent and summed in bfloat16 or wider, within the bound.
A program may use at most 64 MiB of HBM per device.

```python
import jax
import jax.numpy as jnp
from jax import lax

C = 1024
HEADS = 16
HD = 64
W = 16
F = 64
H = 16


def levels(own_key, extent, pieces, low, high):
    level, own = 1.0, jax.random.fold_in(own_key, 6)
    for position, shards_of in pieces:
        steps = jnp.exp(jax.random.uniform(jax.random.fold_in(own, position), (shards_of,), jnp.float32, low / len(pieces), high / len(pieces)))
        level = level * jnp.repeat(steps, extent[position] // shards_of).reshape([-1 if axis == position else 1 for axis in range(len(extent))])
    return level


def gaussian(rng, shape, spread, bound, split=(), held_as=jnp.bfloat16):
    values = jax.random.normal(rng, shape, jnp.float32) * spread
    if len(split) > 0:
        values = levels(rng, shape, split, -0.22, 0.18) * values
    return jnp.clip(values, min=-bound, max=bound).astype(held_as)


def setup_inputs(seed: int = 0) -> dict:
    splits = jax.random.split(jax.random.key(seed), 8)
    latents = gaussian(splits[0], (F, H, W, C), 1.0, 6.0, ((0, 16), (1, 16)))
    conv_gain = jnp.clip(1.0 + 0.18 * jax.random.normal(splits[1], (C,), jnp.float32), 0.1, 1.9)
    spatial_weight = gaussian(splits[2], (3, 3, C, C), (9 * C) ** -0.5, 0.0625, ((2, 16),))
    temporal_weight = gaussian(splits[3], (3, C, C), (3 * C) ** -0.5, 0.109375, ((1, 16),))
    attn_gain = jnp.clip(1.0 + 0.18 * jax.random.normal(splits[4], (C,), jnp.float32), 0.1, 1.9)
    qkv_weight = gaussian(splits[5], (3, C, C), C ** -0.5, 0.1875, ((1, 16),))
    out_weight = gaussian(splits[6], (C, C), C ** -0.5, 0.1875, ((0, 16),))
    return {"latents": latents, "conv_gain": conv_gain, "spatial_weight": spatial_weight, "temporal_weight": temporal_weight, "attn_gain": attn_gain, "qkv_weight": qkv_weight, "out_weight": out_weight}


def rms_scale(values, gain):
    wide = values.astype(jnp.float32)
    return wide * lax.rsqrt(lax.optimization_barrier(jnp.mean(wide * wide, axis=-1, keepdims=True)) + 1e-06) * gain

def dot_trans(left, right):
    return lax.dot_general(left, right, (((1,), (1,)), ((), ())), preferred_element_type=jnp.float32)

def reference(latents, conv_gain, spatial_weight, temporal_weight, attn_gain, qkv_weight, out_weight):
    frames, rows, cols, chans = latents.shape
    normed = rms_scale(latents, conv_gain).astype(jnp.bfloat16)
    padded = jnp.pad(normed, ((0, 0), (1, 1), (1, 1), (0, 0)))
    total = jnp.zeros((frames * rows * cols, chans), jnp.float32)
    for i in range(3):
        for j in range(3):
            window = padded[:, i:i + rows, j:j + cols, :].reshape(-1, chans)
            total = total + dot_trans(window, spatial_weight[i, j])
    activated = jax.nn.silu(total).astype(jnp.bfloat16).reshape(frames, rows, cols, chans)
    before = jnp.roll(activated, 1, axis=0)[0::2].reshape(-1, chans)
    even = activated[0::2].reshape(-1, chans)
    odd = activated[1::2].reshape(-1, chans)
    down32 = jnp.dot(before, temporal_weight[0], preferred_element_type=jnp.float32)
    down32 = down32 + jnp.dot(even, temporal_weight[1], preferred_element_type=jnp.float32)
    down32 = down32 + jnp.dot(odd, temporal_weight[2], preferred_element_type=jnp.float32)
    down = down32.astype(jnp.bfloat16)
    down_normed = rms_scale(down, attn_gain).astype(jnp.bfloat16)
    half = frames // 2
    shape5 = (half, rows, cols, HEADS, HD)
    query = dot_trans(down_normed, qkv_weight[0]).astype(jnp.bfloat16).reshape(shape5)
    key = dot_trans(down_normed, qkv_weight[1]).astype(jnp.bfloat16).reshape(shape5)
    value = dot_trans(down_normed, qkv_weight[2]).astype(jnp.bfloat16).reshape(shape5)
    scores = jnp.einsum('thwnd,shwnd->hwnts', query.astype(jnp.float32), key.astype(jnp.float32)) / jnp.sqrt(jnp.float32(HD))
    probs = jax.nn.softmax(scores, axis=-1).astype(jnp.bfloat16)
    mixed = jnp.einsum('hwnts,shwnd->thwnd', probs.astype(jnp.float32), value.astype(jnp.float32)).astype(jnp.bfloat16)
    projected = jnp.dot(mixed.reshape(-1, chans), out_weight, preferred_element_type=jnp.float32)
    bottom = (down.astype(jnp.float32) + projected).astype(jnp.bfloat16).reshape(half, rows, cols, chans)
    grown = jnp.repeat(bottom, 2, axis=0)
    return (latents.astype(jnp.float32) + grown.astype(jnp.float32)).astype(jnp.bfloat16)
```

```python
import functools

import jax
import jax.numpy as jnp
from jax import lax
from jax.experimental import pallas as pl
from jax.experimental.pallas import tpu as pltpu
from jax.sharding import PartitionSpec as P

HD = 64
COLS = 16
EPS = 1e-06
MESH = pl.DeviceIdType.MESH
F32 = jnp.float32
BF16 = jnp.bfloat16


def dot_trans(left, right):
    return lax.dot_general(left, right, (((1,), (1,)), ((), ())), preferred_element_type=F32)


def dot_plain(left, right):
    return jnp.dot(left, right, preferred_element_type=F32)


def rms(wide, gain):
    return wide * lax.rsqrt(jnp.mean(wide * wide, axis=-1, keepdims=True) + EPS) * gain


def level_kernel(
    orbits,
    spaces,
    lat_hbm,
    cgain_hbm,
    sw_hbm,
    tw_hbm,
    again_hbm,
    qw_hbm,
    ow_hbm,
    bot_ref,
    lat,
    cgain,
    again,
    wsp,
    wtm,
    wqkv,
    wout,
    normed,
    gathered,
    taps,
    act,
    edge,
    part,
    part_in,
    down_own,
    down_twin,
    dnorm,
    qkv_out,
    qkv_in,
    mix_out,
    mix_in,
    proj,
    proj_in,
    local_sem,
    w_send,
    w_recv,
    a_send,
    a_recv,
    e_send,
    e_recv,
    c_send,
    c_recv,
    t_send,
    t_recv,
    d_send,
    d_recv,
    q_send,
    q_recv,
    m_send,
    m_recv,
    f_send,
    f_recv,
):
    chips = spaces // 2
    taus = 2 * orbits
    chans = lat.shape[-1]
    places = spaces * COLS
    share = places // taus
    o = lax.axis_index("orbit")
    s = lax.axis_index("space")
    c = lax.rem(s, 2)
    k = s // 2
    tau = 2 * o + c
    twin = k * 2 + 1 - c

    def send(src, dst, ssem, rsem, to_o, to_s):
        return pltpu.make_async_remote_copy(
            src_ref=src,
            dst_ref=dst,
            send_sem=ssem,
            recv_sem=rsem,
            device_id=(to_o, to_s),
            device_id_type=MESH,
        )

    loads = [
        pltpu.make_async_copy(lat_hbm, lat, local_sem.at[0]),
        pltpu.make_async_copy(cgain_hbm, cgain, local_sem.at[1]),
        pltpu.make_async_copy(again_hbm, again, local_sem.at[2]),
        pltpu.make_async_copy(sw_hbm, wsp.at[:, c], local_sem.at[3]),
        pltpu.make_async_copy(tw_hbm, wtm.at[:, c], local_sem.at[4]),
        pltpu.make_async_copy(qw_hbm, wqkv.at[:, c], local_sem.at[5]),
        pltpu.make_async_copy(ow_hbm, wout.at[c], local_sem.at[6]),
    ]
    for load in loads:
        load.start()

    barrier = pltpu.get_barrier_semaphore()

    def greet_space(d, carry):
        pl.semaphore_signal(
            barrier, inc=1, device_id=(o, lax.rem(s + d, spaces)), device_id_type=MESH
        )
        return carry

    def greet_orbit(d, carry):
        for core in range(2):
            pl.semaphore_signal(
                barrier,
                inc=1,
                device_id=(lax.rem(o + d, orbits), 2 * k + core),
                device_id_type=MESH,
            )
        return carry

    lax.fori_loop(1, spaces, greet_space, 0)
    lax.fori_loop(1, orbits, greet_orbit, 0)
    loads[0].wait()
    loads[1].wait()
    row = rms(lat[...].astype(F32).reshape(4 * COLS, chans), cgain[...]).astype(BF16)
    normed[...] = row.reshape(2, 2, COLS, chans)
    pl.semaphore_wait(barrier, spaces - 1 + 2 * (orbits - 1))

    weights = [
        send(sw_hbm, wsp.at[:, c], w_send.at[0], w_recv.at[0], o, twin),
        send(tw_hbm, wtm.at[:, c], w_send.at[1], w_recv.at[1], o, twin),
        send(qw_hbm, wqkv.at[:, c], w_send.at[2], w_recv.at[2], o, twin),
        send(ow_hbm, wout.at[c], w_send.at[3], w_recv.at[3], o, twin),
    ]

    def a_copy(d):
        to = lax.rem(s + d, spaces)
        return send(
            normed.at[lax.rem(to, 2)], gathered.at[s], a_send.at[d], a_recv.at[s], o, to
        )

    def a_start(d, carry):
        a_copy(d).start()
        return carry

    lax.fori_loop(1, spaces, a_start, 0)
    for copy in weights:
        copy.start()
    gathered[s] = normed[c]

    def a_wait(d, carry):
        frm = lax.rem(s + d, spaces)
        send(
            normed.at[0], gathered.at[frm], a_send.at[d], a_recv.at[frm], o, frm
        ).wait_recv()
        return carry

    loads[3].wait()
    weights[0].wait_recv()
    lax.fori_loop(1, spaces, a_wait, 0)

    step_rows = 4
    step = step_rows * 2 * COLS

    def conv_step(i, carry):
        rows = gathered[pl.ds(i * step_rows, step_rows)].reshape(step, chans)
        start = pl.multiple_of(2 * COLS + i * step, 2 * COLS)
        taps[pl.ds(start, step), :] = dot_trans(rows, wsp[...].reshape(9 * 128, chans))
        return carry

    lax.fori_loop(0, spaces // step_rows, conv_step, 0)
    span = spaces * 2 * COLS
    zero_rows = jnp.zeros((2 * COLS, 9 * 128), F32)
    taps[0 : 2 * COLS, :] = zero_rows
    taps[2 * COLS + span :, :] = zero_rows

    col = lax.rem(lax.broadcasted_iota(jnp.int32, (step, 128), 0), COLS)

    def join_step(i, carry):
        base = i * step

        def column(j):
            total = None
            for tap in range(3):
                start = pl.multiple_of(base + tap * 2 * COLS, 2 * COLS)
                lane = (tap * 3 + j) * 128
                term = taps[pl.ds(start, step), lane : lane + 128]
                total = term if total is None else total + term
            return total

        left = jnp.where(col == 0, 0.0, pltpu.roll(column(0), 1, 0))
        right = jnp.where(col == COLS - 1, 0.0, pltpu.roll(column(2), step - 1, 0))
        total = left + column(1) + right
        total = total * (1.0 / (1.0 + jnp.exp(-total)))
        total = total.astype(BF16).reshape(step_rows, 2, COLS, 128)
        for view in range(2):
            act[view, pl.ds(i * step_rows, step_rows)] = total[:, view]
        return carry

    lax.fori_loop(0, spaces // step_rows, join_step, 0)

    after = lax.rem(tau + 1, taus)
    edge_copy = send(
        act.at[1], edge, e_send.at[0], e_recv.at[0], after // 2, 2 * k + lax.rem(after, 2)
    )
    edge_copy.start()
    loads[4].wait()
    weights[1].wait_recv()
    edge_copy.wait_recv()

    half = places // 2
    half_chips = chips // 2

    def flat(ref):
        return ref[...].reshape(places, 128)

    before, even, odd = flat(edge), act[0].reshape(places, 128), act[1].reshape(places, 128)
    total = dot_plain(before, wtm[0].reshape(128, chans))
    total = total + dot_plain(even, wtm[1].reshape(128, chans))
    total = total + dot_plain(odd, wtm[2].reshape(128, chans))
    part[...] = total.astype(BF16).reshape(chips, 2 * COLS, chans)

    def c_copy(d):
        to = lax.rem(k + d, chips)
        return send(
            part.at[to], part_in.at[k], c_send.at[d], c_recv.at[k], o, 2 * to + c
        )

    def c_start(d, carry):
        c_copy(d).start()
        return carry

    lax.fori_loop(1, chips, c_start, 0)
    part_in[k] = part[k]

    def c_wait(d, carry):
        frm = lax.rem(k + d, chips)
        send(
            part.at[0], part_in.at[frm], c_send.at[d], c_recv.at[frm], o, 2 * frm + c
        ).wait_recv()
        return carry

    lax.fori_loop(1, chips, c_wait, 0)
    total = part_in[0].astype(F32)
    for i in range(1, chips):
        total = total + part_in[i].astype(F32)
    down = total.astype(BF16)
    down_own[...] = down.reshape(2, COLS, chans)
    loads[2].wait()
    dnorm[k] = rms(down.astype(F32), again[...]).astype(BF16)

    def d_copy(d):
        to = lax.rem(k + d, chips)
        return send(
            dnorm.at[k], dnorm.at[k], d_send.at[d], d_recv.at[k], o, 2 * to + c
        )

    def d_start(d, carry):
        d_copy(d).start()
        return carry

    lax.fori_loop(1, chips, d_start, 0)
    twin_copy = send(
        down_own.at[1 - c], down_twin, t_send.at[0], t_recv.at[0], o, twin
    )
    twin_copy.start()

    def d_wait(d, carry):
        frm = lax.rem(k + d, chips)
        send(
            dnorm.at[frm], dnorm.at[frm], d_send.at[d], d_recv.at[frm], o, 2 * frm + c
        ).wait_recv()
        return carry

    loads[5].wait()
    weights[2].wait_recv()
    lax.fori_loop(1, chips, d_wait, 0)
    qkv = dot_trans(dnorm[...].reshape(places, chans), wqkv[...].reshape(384, chans))
    qkv_out[...] = qkv.reshape(taus, share, 384).astype(BF16)

    def q_copy(d):
        to = lax.rem(tau + d, taus)
        return send(
            qkv_out.at[to],
            qkv_in.at[tau],
            q_send.at[d],
            q_recv.at[tau],
            to // 2,
            2 * k + lax.rem(to, 2),
        )

    def q_start(d, carry):
        q_copy(d).start()
        return carry

    lax.fori_loop(1, taus, q_start, 0)
    qkv_in[tau] = qkv_out[tau]

    def q_wait(d, carry):
        frm = lax.rem(tau + d, taus)
        send(
            qkv_out.at[0], qkv_in.at[frm], q_send.at[d], q_recv.at[frm], o, s
        ).wait_recv()
        return carry

    lax.fori_loop(1, taus, q_wait, 0)
    every = qkv_in[...].astype(F32).reshape(places, 384)
    query = every[:, :128]
    key = every[:, 128:256].astype(BF16)
    value = every[:, 256:].astype(BF16)
    lane = lax.broadcasted_iota(jnp.int32, (places, 128), 1)
    left_place = lax.rem(lax.broadcasted_iota(jnp.int32, (places, places), 0), share)
    right_place = lax.rem(lax.broadcasted_iota(jnp.int32, (places, places), 1), share)
    same = left_place == right_place
    mixes = []
    for head in range(2):
        mine = (lane // HD) == head
        scores = dot_trans(jnp.where(mine, query, 0.0).astype(BF16), key) * (HD**-0.5)
        scores = jnp.where(same, scores, -jnp.inf)
        top = jnp.max(scores, axis=-1, keepdims=True)
        grown = jnp.exp(scores - top)
        probs = (grown / jnp.sum(grown, axis=-1, keepdims=True)).astype(BF16)
        mixes.append(dot_plain(probs, value))
    mixed = jnp.where(lane < HD, mixes[0], mixes[1])
    mix_out[...] = mixed.reshape(taus, share, 128).astype(BF16)

    def m_copy(d):
        to = lax.rem(tau + d, taus)
        return send(
            mix_out.at[to],
            mix_in.at[tau],
            m_send.at[d],
            m_recv.at[tau],
            to // 2,
            2 * k + lax.rem(to, 2),
        )

    def m_start(d, carry):
        m_copy(d).start()
        return carry

    lax.fori_loop(1, taus, m_start, 0)
    mix_in[tau] = mix_out[tau]

    def m_wait(d, carry):
        frm = lax.rem(tau + d, taus)
        send(
            mix_out.at[0], mix_in.at[frm], m_send.at[d], m_recv.at[frm], o, s
        ).wait_recv()
        return carry

    loads[6].wait()
    weights[3].wait_recv()
    lax.fori_loop(1, taus, m_wait, 0)
    mixed_all = mix_in[...].astype(F32).reshape(places, 128).astype(BF16)
    projected = dot_plain(mixed_all, wout[...].reshape(128, chans))
    proj[...] = projected.astype(BF16).reshape(spaces, COLS, chans)

    def f_copy(d):
        to = lax.rem(s + d, spaces)
        return send(proj.at[to], proj_in.at[s], f_send.at[d], f_recv.at[s], o, to)

    def f_start(d, carry):
        f_copy(d).start()
        return carry

    lax.fori_loop(1, spaces, f_start, 0)
    proj_in[s] = proj[s]

    def f_wait(d, carry):
        frm = lax.rem(s + d, spaces)
        send(
            proj.at[0], proj_in.at[frm], f_send.at[d], f_recv.at[frm], o, frm
        ).wait_recv()
        return carry

    lax.fori_loop(1, spaces, f_wait, 0)
    twin_copy.wait_recv()
    own_half = down_own[c].astype(F32)
    other_half = down_twin[...].astype(F32)
    for t in range(2):
        total = proj_in[t].astype(F32)
        for i in range(1, chips):
            total = total + proj_in[2 * i + t].astype(F32)
        base = jnp.where(c == t, own_half, other_half)
        bot_ref[t] = (base + total).astype(BF16)

    for copy in weights:
        copy.wait_send()
    edge_copy.wait_send()
    twin_copy.wait_send()

    def drain(make):
        def one(d, carry):
            make(d).wait_send()
            return carry

        return one

    lax.fori_loop(1, spaces, drain(a_copy), 0)
    lax.fori_loop(1, chips, drain(c_copy), 0)
    lax.fori_loop(1, chips, drain(d_copy), 0)
    lax.fori_loop(1, taus, drain(q_copy), 0)
    lax.fori_loop(1, taus, drain(m_copy), 0)
    lax.fori_loop(1, spaces, drain(f_copy), 0)


def body(latents, conv_gain, spatial_weight, temporal_weight, attn_gain, qkv_weight, out_weight):
    orbits, spaces = lax.axis_size("orbit"), lax.axis_size("space")
    chans = latents.shape[-1]
    chips, taus = spaces // 2, 2 * orbits
    places = spaces * COLS
    share = places // taus
    vmem = pltpu.VMEM
    sem = pltpu.SemaphoreType.DMA
    bottom = pl.pallas_call(
        functools.partial(level_kernel, orbits, spaces),
        out_shape=jax.ShapeDtypeStruct((2, COLS, chans), BF16),
        in_specs=[pl.BlockSpec(memory_space=pl.ANY)] * 7,
        out_specs=pl.BlockSpec(memory_space=pltpu.VMEM),
        scratch_shapes=[
            vmem((4, 1, COLS, chans), BF16),
            vmem((1, chans), F32),
            vmem((1, chans), F32),
            vmem((9, 2, 64, chans), BF16),
            vmem((3, 2, 64, chans), BF16),
            vmem((3, 2, 64, chans), BF16),
            vmem((2, 64, chans), BF16),
            vmem((2, 2, COLS, chans), BF16),
            vmem((spaces, 2, COLS, chans), BF16),
            vmem(((spaces + 2) * 2 * COLS, 9 * 128), F32),
            vmem((2, spaces, COLS, 128), BF16),
            vmem((spaces, COLS, 128), BF16),
            vmem((chips, 2 * COLS, chans), BF16),
            vmem((chips, 2 * COLS, chans), BF16),
            vmem((2, COLS, chans), BF16),
            vmem((COLS, chans), BF16),
            vmem((chips, 2 * COLS, chans), BF16),
            vmem((taus, share, 384), BF16),
            vmem((taus, share, 384), BF16),
            vmem((taus, share, 128), BF16),
            vmem((taus, share, 128), BF16),
            vmem((spaces, COLS, chans), BF16),
            vmem((spaces, COLS, chans), BF16),
            sem((7,)),
            sem((4,)),
            sem((4,)),
            sem((spaces,)),
            sem((spaces,)),
            sem((1,)),
            sem((1,)),
            sem((chips,)),
            sem((chips,)),
            sem((1,)),
            sem((1,)),
            sem((chips,)),
            sem((chips,)),
            sem((taus,)),
            sem((taus,)),
            sem((taus,)),
            sem((taus,)),
            sem((spaces,)),
            sem((spaces,)),
        ],
        compiler_params=pltpu.CompilerParams(
            collective_id=0, has_side_effects=True, vmem_limit_bytes=40 * 2**20
        ),
    )(
        latents,
        conv_gain.reshape(1, chans),
        spatial_weight.reshape(9, 64, chans),
        temporal_weight,
        attn_gain.reshape(1, chans),
        qkv_weight,
        out_weight,
    )
    grown = jnp.repeat(bottom, 2, axis=0)[:, None]
    return (latents.astype(F32) + grown.astype(F32)).astype(BF16)


def solution(mesh):
    return jax.shard_map(
        body,
        mesh=mesh,
        in_specs=(
            P("orbit", "space", None, None),
            P(),
            P(None, None, "space", None),
            P(None, "space", None),
            P(),
            P(None, "space", None),
            P("space", None),
        ),
        out_specs=P("orbit", "space", None, None),
        check_vma=False,
    )
```

```python
import functools

import jax
import jax.numpy as jnp
from jax import lax
from jax.experimental import pallas as pl
from jax.experimental.pallas import tpu as pltpu
from jax.sharding import PartitionSpec as P

HD = 64
COLS = 16
QUARTERS = 4
EPS = 1e-06
MESH = pl.DeviceIdType.MESH
F32 = jnp.float32
BF16 = jnp.bfloat16


def dot_trans(left, right):
    return lax.dot_general(left, right, (((1,), (1,)), ((), ())), preferred_element_type=F32)


def dot_plain(left, right):
    return jnp.dot(left, right, preferred_element_type=F32)


def rms(wide, gain):
    return wide * lax.rsqrt(jnp.mean(wide * wide, axis=-1, keepdims=True) + EPS) * gain


def level_kernel(
    orbits,
    spaces,
    lat_hbm,
    cgain_hbm,
    sw_hbm,
    tw_hbm,
    again_hbm,
    qw_hbm,
    ow_hbm,
    bot_ref,
    lat,
    cgain,
    again,
    wsp,
    wtm,
    wqkv,
    wout,
    normed,
    gathered,
    taps,
    act,
    edge,
    part,
    part_in,
    down,
    d_out,
    d_in,
    proj,
    f_in,
    local_sem,
    ring_sem,
    w_send,
    w_recv,
    y_send,
    y_recv,
    a_send,
    a_recv,
    e_send,
    e_recv,
    c_send,
    c_recv,
    d_send,
    d_recv,
    f_send,
    f_recv,
):
    xs = spaces // 4
    chips = spaces // 2
    taus = 2 * orbits
    chans = lat.shape[-1]
    places = spaces * COLS
    pairs = 8 * orbits
    o = lax.axis_index("orbit")
    s = lax.axis_index("space")
    c = lax.rem(s, 2)
    k = s // 2
    y = lax.rem(k, 2)
    x = s // 4
    slot = lax.rem(s, 4)
    tau = 2 * o + c
    twin = s + 1 - 2 * c
    beside = s + 2 - 4 * y
    across = lax.rem(o + orbits // 2, orbits)

    def worker(of_x, of_c, q):
        if xs == 1:
            return q, of_c
        return (of_x // 2) * 8 + of_c * 4 + q, lax.rem(of_x, 2)

    if xs == 1:
        wx, wc, wq = 0, c, o
    else:
        wx, wc, wq = (o // 8) * 2 + c, lax.rem(o, 8) // 4, lax.rem(o, 4)
    served = wx * 4 + y * 2 + wc

    def send(src, dst, ssem, rsem, to_o, to_s):
        return pltpu.make_async_remote_copy(
            src_ref=src,
            dst_ref=dst,
            send_sem=ssem,
            recv_sem=rsem,
            device_id=(to_o, to_s),
            device_id_type=MESH,
        )

    sent = []

    def each(count, make, what, first=0):
        def one(d, carry):
            what(make(d))
            return carry

        lax.fori_loop(first, count, one, 0)

    loads = [
        pltpu.make_async_copy(lat_hbm, lat, local_sem.at[0]),
        pltpu.make_async_copy(cgain_hbm, cgain, local_sem.at[1]),
        pltpu.make_async_copy(sw_hbm, wsp.at[:, c], local_sem.at[2]),
        pltpu.make_async_copy(tw_hbm, wtm.at[:, c], local_sem.at[3]),
        pltpu.make_async_copy(again_hbm, again, local_sem.at[4]),
        pltpu.make_async_copy(qw_hbm, wqkv.at[:, slot], local_sem.at[5]),
        pltpu.make_async_copy(ow_hbm, wout.at[slot], local_sem.at[6]),
    ]
    for load in loads:
        load.start()

    barrier = pltpu.get_barrier_semaphore()

    def signal(sem, to_o, to_s):
        pl.semaphore_signal(sem, inc=1, device_id=(to_o, to_s), device_id_type=MESH)

    def greet(d, carry):
        signal(barrier, o, lax.rem(s + d, spaces))
        return carry

    lax.fori_loop(1, spaces, greet, 0)
    signal(barrier, lax.rem(o + 1, orbits), s)
    signal(barrier, lax.rem(o + orbits - 1, orbits), s)
    beside_twin = beside + 1 - 2 * c
    signal(barrier, across, beside)
    signal(barrier, across, beside_twin)

    rounds = []
    distance = 1
    while distance < orbits:
        rounds.append(distance)
        distance *= 2

    def round_signal(i):
        signal(ring_sem.at[i], lax.rem(o + rounds[i], orbits), s)
        if 2 * rounds[i] != orbits:
            signal(ring_sem.at[i], lax.rem(o + orbits - rounds[i], orbits), s)

    def round_wait(i):
        pl.semaphore_wait(ring_sem.at[i], 1 if 2 * rounds[i] == orbits else 2)

    last_round = len(rounds) - 1

    loads[0].wait()
    loads[1].wait()
    row = rms(lat[...].astype(F32).reshape(4 * COLS, chans), cgain[...]).astype(BF16)
    normed[...] = row.reshape(4, COLS, chans)
    pl.semaphore_wait(barrier, spaces - 1 + 4)

    weights = [
        send(sw_hbm, wsp.at[:, c], w_send.at[0], w_recv.at[0], o, twin),
        send(tw_hbm, wtm.at[:, c], w_send.at[1], w_recv.at[1], o, twin),
        send(qw_hbm, wqkv.at[:, slot], w_send.at[2], w_recv.at[2], o, twin),
        send(ow_hbm, wout.at[slot], w_send.at[3], w_recv.at[3], o, twin),
    ]
    for core in range(2):
        there = beside - c + core
        weights.append(
            send(
                qw_hbm, wqkv.at[:, slot], y_send.at[core], y_recv.at[2 * c], across, there
            )
        )
        weights.append(
            send(
                ow_hbm, wout.at[slot], y_send.at[2 + core], y_recv.at[2 * c + 1], across, there
            )
        )

    def a_copy(v):
        def make(d):
            to = lax.rem(s + d, spaces)
            return send(
                normed.at[2 * lax.rem(to, 2) + v],
                gathered.at[v, s],
                a_send.at[v, d],
                a_recv.at[v, s],
                o,
                to,
            )

        return make

    def a_from(v):
        def make(d):
            frm = lax.rem(s + d, spaces)
            return send(
                normed.at[0], gathered.at[v, frm], a_send.at[v, d], a_recv.at[v, frm], o, frm
            )

        return make

    weights[0].start()
    for v in (1, 0):
        each(spaces, a_copy(v), lambda copy: copy.start(), 1)
        sent.append((spaces, a_copy(v), 1))
        gathered[v, s] = normed[2 * c + v]
    for copy in weights[1:]:
        copy.start()
    round_signal(0)

    zero_rows = jnp.zeros((COLS, 9 * 128), F32)
    taps[0:COLS, :] = zero_rows
    taps[COLS + places :, :] = zero_rows
    step = places // 2
    col = lax.rem(lax.broadcasted_iota(jnp.int32, (step, 128), 0), COLS)

    def convolve(v):
        rows = gathered[v].reshape(places, chans)
        taps[COLS : COLS + places, :] = dot_trans(rows, wsp[...].reshape(9 * 128, chans))
        for part_of in range(2):
            base = part_of * step

            def column(j):
                total = None
                for tap in range(3):
                    start = base + tap * COLS
                    lane = (tap * 3 + j) * 128
                    term = taps[start : start + step, lane : lane + 128]
                    total = term if total is None else total + term
                return total

            left = jnp.where(col == 0, 0.0, pltpu.roll(column(0), 1, 0))
            right = jnp.where(col == COLS - 1, 0.0, pltpu.roll(column(2), step - 1, 0))
            total = left + column(1) + right
            total = total * (1.0 / (1.0 + jnp.exp(-total)))
            act[v, base : base + step] = total.astype(BF16)

    round_wait(0)
    round_signal(1)
    loads[2].wait()
    weights[0].wait_recv()
    each(spaces, a_from(1), lambda copy: copy.wait_recv(), 1)
    convolve(1)
    after = lax.rem(tau + 1, taus)
    edge_copy = send(
        act.at[1], edge, e_send.at[0], e_recv.at[0], after // 2, 2 * k + lax.rem(after, 2)
    )
    edge_copy.start()
    loads[3].wait()
    weights[1].wait_recv()
    round_wait(1)
    for i in range(2, last_round):
        round_signal(i)
        round_wait(i)
    if last_round > 1:
        round_signal(last_round)
    each(spaces, a_from(0), lambda copy: copy.wait_recv(), 1)
    convolve(0)
    total = dot_plain(act[0], wtm[1].reshape(128, chans))
    total = total + dot_plain(act[1], wtm[2].reshape(128, chans))
    edge_copy.wait_recv()
    total = total + dot_plain(edge[...], wtm[0].reshape(128, chans))
    part[...] = total.reshape(spaces, 2, 8, chans).astype(BF16)

    def c_copy(half):
        def make(d):
            to = lax.rem(s + d, spaces)
            return send(
                part.at[to, half],
                part_in.at[half, k, c],
                c_send.at[half, d],
                c_recv.at[half, s],
                o,
                to,
            )

        return make

    def c_from(half):
        def make(d):
            frm = lax.rem(s + d, spaces)
            return send(
                part.at[0, half],
                part_in.at[half, frm // 2, lax.rem(frm, 2)],
                c_send.at[half, d],
                c_recv.at[half, frm],
                o,
                frm,
            )

        return make

    for half in range(2):
        each(spaces, c_copy(half), lambda copy: copy.start(), 1)
        sent.append((spaces, c_copy(half), 1))
        part_in[half, k, c] = part[s, half]

    if last_round > 1:
        round_wait(last_round)
    loads[4].wait()
    upper = lax.broadcasted_iota(jnp.int32, (8, chans), 0) < 4

    def d_target(q, to_x):
        to_o, to_c = worker(x, c, q)
        return to_o, to_x * 4 + y * 2 + to_c

    def d_copy(q, to_x):
        to_o, to_s = d_target(q, to_x)
        i = q * xs + to_x
        return send(d_out.at[q], d_in.at[o], d_send.at[i], d_recv.at[o], to_o, to_s)

    def is_here(to_o, to_s):
        return jnp.logical_and(to_o == o, to_s == s)

    for half in range(2):
        each(spaces, c_from(half), lambda copy: copy.wait_recv(), 1)
        if half == 1:
            pass
        total = jnp.sum(part_in[half].astype(F32), axis=0)
        rounded = total.astype(BF16)
        down[half] = rounded
        wide = rms(rounded.astype(F32), again[...])
        first, second = wide[0], wide[1]
        d_out[2 * half] = jnp.where(upper, first, pltpu.roll(second, 4, 0)).astype(BF16)
        d_out[2 * half + 1] = jnp.where(upper, pltpu.roll(first, 4, 0), second).astype(BF16)
        for q in (2 * half, 2 * half + 1):
            for to_x in range(xs):
                here = is_here(*d_target(q, to_x))

                @pl.when(here)
                def _(q=q):
                    pltpu.make_async_copy(d_out.at[q], d_in.at[o], d_recv.at[o]).start()

                @pl.when(jnp.logical_not(here))
                def _(q=q, to_x=to_x):
                    d_copy(q, to_x).start()

    weights[2].wait_recv()
    weights[3].wait_recv()
    for core in range(2):
        theirs = 2 - 2 * y + core
        send(
            qw_hbm, wqkv.at[:, theirs], y_send.at[0], y_recv.at[2 * core], across, beside
        ).wait_recv()
        send(
            ow_hbm, wout.at[theirs], y_send.at[0], y_recv.at[2 * core + 1], across, beside
        ).wait_recv()
    loads[5].wait()
    loads[6].wait()

    def d_from(i):
        return send(d_out.at[0], d_in.at[i], d_send.at[0], d_recv.at[i], i, served)

    each(orbits, d_from, lambda copy: copy.wait_recv())
    rows = d_in[...].astype(F32).reshape(pairs, chans).astype(BF16)
    qkv = dot_trans(rows, wqkv[...].reshape(3 * 4 * HD, chans))
    lane = lax.broadcasted_iota(jnp.int32, (pairs, 128), 1)
    left_place = lax.rem(lax.broadcasted_iota(jnp.int32, (pairs, pairs), 0), QUARTERS)
    right_place = lax.rem(lax.broadcasted_iota(jnp.int32, (pairs, pairs), 1), QUARTERS)
    same = left_place == right_place
    mixes = []
    for block in range(2):
        at = block * 128
        query = qkv[:, at : at + 128]
        key = qkv[:, 256 + at : 256 + at + 128].astype(BF16)
        value = qkv[:, 512 + at : 512 + at + 128].astype(BF16)
        heads = []
        for head in range(2):
            mine = (lane // HD) == head
            scores = dot_trans(jnp.where(mine, query, 0.0).astype(BF16), key) * (HD**-0.5)
            scores = jnp.where(same, scores, -jnp.inf)
            top = jnp.max(scores, axis=-1, keepdims=True)
            grown = jnp.exp(scores - top)
            probs = (grown / jnp.sum(grown, axis=-1, keepdims=True)).astype(BF16)
            heads.append(dot_plain(probs, value))
        mixes.append(jnp.where(lane < HD, heads[0], heads[1]).astype(BF16))
    wide_out = wout[...].reshape(4 * HD, chans)
    projected = dot_plain(mixes[0], wide_out[:128]) + dot_plain(mixes[1], wide_out[128:])
    proj[...] = projected.reshape(orbits, 8, chans).astype(BF16)

    def f_copy(i):
        return send(proj.at[i], f_in.at[x, wq], f_send.at[i], f_recv.at[4 * x + wq], i, served)

    def f_start(i, carry):
        here = is_here(i, served)

        @pl.when(here)
        def _():
            pltpu.make_async_copy(proj.at[i], f_in.at[x, wq], f_recv.at[4 * x + wq]).start()

        @pl.when(jnp.logical_not(here))
        def _():
            f_copy(i).start()

        return carry

    lax.fori_loop(0, orbits, f_start, 0)

    def f_from(i):
        return send(
            proj.at[0], f_in.at[i // 4, lax.rem(i, 4)], f_send.at[0], f_recv.at[i], o, twin
        )

    each(4 * xs, f_from, lambda copy: copy.wait_recv())
    for half in range(2):
        low = jnp.sum(f_in[:, 2 * half].astype(F32), axis=0)
        high = jnp.sum(f_in[:, 2 * half + 1].astype(F32), axis=0)
        first = jnp.where(upper, low, pltpu.roll(high, 4, 0))
        second = jnp.where(upper, pltpu.roll(low, 4, 0), high)
        bot_ref[0, half] = (down[half, 0].astype(F32) + first).astype(BF16)
        bot_ref[1, half] = (down[half, 1].astype(F32) + second).astype(BF16)

    for copy in weights:
        copy.wait_send()
    edge_copy.wait_send()
    for count, make, first in sent:
        each(count, make, lambda copy: copy.wait_send(), first)

    for q in range(4):
        for to_x in range(xs):

            @pl.when(jnp.logical_not(is_here(*d_target(q, to_x))))
            def _(q=q, to_x=to_x):
                d_copy(q, to_x).wait_send()

    def f_drain(i, carry):
        @pl.when(jnp.logical_not(is_here(i, served)))
        def _():
            f_copy(i).wait_send()

        return carry

    lax.fori_loop(0, orbits, f_drain, 0)


def body(latents, conv_gain, spatial_weight, temporal_weight, attn_gain, qkv_weight, out_weight):
    orbits, spaces = lax.axis_size("orbit"), lax.axis_size("space")
    chans = latents.shape[-1]
    chips, xs = spaces // 2, spaces // 4
    places = spaces * COLS
    vmem = pltpu.VMEM
    sem = pltpu.SemaphoreType.DMA
    bottom = pl.pallas_call(
        functools.partial(level_kernel, orbits, spaces),
        out_shape=jax.ShapeDtypeStruct((2, 2, 8, chans), BF16),
        in_specs=[pl.BlockSpec(memory_space=pltpu.HBM)] * 7,
        out_specs=pl.BlockSpec(memory_space=pltpu.VMEM),
        scratch_shapes=[
            vmem((4, 1, COLS, chans), BF16),
            vmem((1, chans), F32),
            vmem((1, chans), F32),
            vmem((9, 2, 64, chans), BF16),
            vmem((3, 2, 64, chans), BF16),
            vmem((3, 4, 64, chans), BF16),
            vmem((4, 64, chans), BF16),
            vmem((4, COLS, chans), BF16),
            vmem((2, spaces, COLS, chans), BF16),
            vmem((places + 2 * COLS, 9 * 128), F32),
            vmem((2, places, 128), BF16),
            vmem((places, 128), BF16),
            vmem((spaces, 2, 8, chans), BF16),
            vmem((2, chips, 2, 8, chans), BF16),
            vmem((2, 2, 8, chans), BF16),
            vmem((QUARTERS, 8, chans), BF16),
            vmem((orbits, 8, chans), BF16),
            vmem((orbits, 8, chans), BF16),
            vmem((xs, QUARTERS, 8, chans), BF16),
            sem((7,)),
            pltpu.SemaphoreType.REGULAR((4,)),
            sem((4,)),
            sem((4,)),
            sem((4,)),
            sem((4,)),
            sem((2, spaces)),
            sem((2, spaces)),
            sem((1,)),
            sem((1,)),
            sem((2, spaces)),
            sem((2, spaces)),
            sem((spaces,)),
            sem((orbits,)),
            sem((orbits,)),
            sem((spaces,)),
        ],
        compiler_params=pltpu.CompilerParams(
            collective_id=0, has_side_effects=True, vmem_limit_bytes=40 * 2**20
        ),
    )(
        *(
            pltpu.with_memory_space_constraint(array, pltpu.HBM)
            for array in (
                latents,
                conv_gain.reshape(1, chans),
                spatial_weight.reshape(9, 64, chans),
                temporal_weight,
                attn_gain.reshape(1, chans),
                qkv_weight,
                out_weight,
            )
        )
    )
    grown = jnp.repeat(bottom.reshape(2, COLS, chans), 2, axis=0)[:, None]
    return (latents.astype(F32) + grown.astype(F32)).astype(BF16)


def solution(mesh):
    return jax.shard_map(
        body,
        mesh=mesh,
        in_specs=(
            P("orbit", "space", None, None),
            P(),
            P(None, None, "space", None),
            P(None, "space", None),
            P(),
            P(None, "space", None),
            P("space", None),
        ),
        out_specs=P("orbit", "space", None, None),
        check_vma=False,
    )
```

```python
import functools

import jax
import jax.numpy as jnp
from jax import lax
from jax.experimental import pallas as pl
from jax.experimental.pallas import tpu as pltpu
from jax.sharding import PartitionSpec as P

HD = 64
COLS = 16
QUARTERS = 4
EPS = 1e-06
MESH = pl.DeviceIdType.MESH
F32 = jnp.float32
BF16 = jnp.bfloat16


def dot_trans(left, right):
    return lax.dot_general(left, right, (((1,), (1,)), ((), ())), preferred_element_type=F32)


def dot_plain(left, right):
    return jnp.dot(left, right, preferred_element_type=F32)


def rms(wide, gain):
    return wide * lax.rsqrt(jnp.mean(wide * wide, axis=-1, keepdims=True) + EPS) * gain


def level_kernel(
    orbits,
    spaces,
    lat_hbm,
    cgain_hbm,
    sw_hbm,
    tw_hbm,
    again_hbm,
    qw_hbm,
    ow_hbm,
    bot_ref,
    lat,
    cgain,
    again,
    wsp,
    wtm,
    wqkv,
    wout,
    normed,
    gathered,
    taps,
    act,
    edge,
    part,
    part_in,
    down,
    d_out,
    d_in,
    proj,
    f_in,
    local_sem,
    ring_sem,
    w_send,
    w_recv,
    y_send,
    y_recv,
    a_send,
    a_recv,
    e_send,
    e_recv,
    c_send,
    c_recv,
    d_send,
    d_recv,
    f_send,
    f_recv,
):
    xs = spaces // 4
    chips = spaces // 2
    taus = 2 * orbits
    chans = lat.shape[-1]
    places = spaces * COLS
    pairs = 8 * orbits
    o = lax.axis_index("orbit")
    s = lax.axis_index("space")
    c = lax.rem(s, 2)
    k = s // 2
    y = lax.rem(k, 2)
    x = s // 4
    slot = lax.rem(s, 4)
    tau = 2 * o + c
    twin = s + 1 - 2 * c
    beside = s + 2 - 4 * y
    across = lax.rem(o + orbits // 2, orbits)

    def worker(of_x, of_c, q):
        if xs == 1:
            return q, of_c
        return lax.rem(of_x // 2 + q, xs // 2) * 8 + of_c * 4 + q, lax.rem(of_x, 2)

    if xs == 1:
        wx, wc, wq = 0, c, o
    else:
        wc, wq = lax.rem(o, 8) // 4, lax.rem(o, 4)
        wx = lax.rem(o // 8 + xs // 2 * QUARTERS - wq, xs // 2) * 2 + c
    served = wx * 4 + y * 2 + wc

    def send(src, dst, ssem, rsem, to_o, to_s):
        return pltpu.make_async_remote_copy(
            src_ref=src,
            dst_ref=dst,
            send_sem=ssem,
            recv_sem=rsem,
            device_id=(to_o, to_s),
            device_id_type=MESH,
        )

    sent = []

    def each(count, make, what, first=0):
        def one(d, carry):
            what(make(d))
            return carry

        lax.fori_loop(first, count, one, 0)

    loads = [
        pltpu.make_async_copy(lat_hbm, lat, local_sem.at[0]),
        pltpu.make_async_copy(cgain_hbm, cgain, local_sem.at[1]),
        pltpu.make_async_copy(sw_hbm, wsp.at[:, c], local_sem.at[2]),
        pltpu.make_async_copy(tw_hbm, wtm.at[:, c], local_sem.at[3]),
        pltpu.make_async_copy(again_hbm, again, local_sem.at[4]),
        pltpu.make_async_copy(qw_hbm, wqkv.at[:, slot], local_sem.at[5]),
        pltpu.make_async_copy(ow_hbm, wout.at[slot], local_sem.at[6]),
    ]
    barrier = pltpu.get_barrier_semaphore()

    def signal(sem, to_o, to_s):
        pl.semaphore_signal(sem, inc=1, device_id=(to_o, to_s), device_id_type=MESH)

    def greet(d, carry):
        signal(barrier, o, lax.rem(s + d, spaces))
        return carry

    lax.fori_loop(1, spaces, greet, 0)
    signal(barrier, lax.rem(o + 1, orbits), s)
    signal(barrier, lax.rem(o + orbits - 1, orbits), s)
    beside_twin = beside + 1 - 2 * c
    signal(barrier, across, beside)
    signal(barrier, across, beside_twin)
    for load in loads:
        load.start()

    rounds = []
    distance = 1
    while distance < orbits:
        rounds.append(distance)
        distance *= 2

    def round_signal(i):
        signal(ring_sem.at[i], lax.rem(o + rounds[i], orbits), s)
        if 2 * rounds[i] != orbits:
            signal(ring_sem.at[i], lax.rem(o + orbits - rounds[i], orbits), s)

    def round_wait(i):
        pl.semaphore_wait(ring_sem.at[i], 1 if 2 * rounds[i] == orbits else 2)

    last_round = len(rounds) - 1

    loads[0].wait()
    loads[1].wait()
    row = rms(lat[...].astype(F32).reshape(4 * COLS, chans), cgain[...]).astype(BF16)
    normed[...] = row.reshape(4, COLS, chans)
    pl.semaphore_wait(barrier, spaces - 1 + 4)

    weights = [
        send(sw_hbm, wsp.at[:, c], w_send.at[0], w_recv.at[0], o, twin),
        send(tw_hbm, wtm.at[:, c], w_send.at[1], w_recv.at[1], o, twin),
        send(qw_hbm, wqkv.at[:, slot], w_send.at[2], w_recv.at[2], o, twin),
        send(ow_hbm, wout.at[slot], w_send.at[3], w_recv.at[3], o, twin),
    ]
    for core in range(2):
        there = beside - c + core
        weights.append(
            send(
                qw_hbm, wqkv.at[:, slot], y_send.at[core], y_recv.at[2 * c], across, there
            )
        )
        weights.append(
            send(
                ow_hbm, wout.at[slot], y_send.at[2 + core], y_recv.at[2 * c + 1], across, there
            )
        )

    peers = [lax.rem(x + d, xs) * 4 + 2 * y for d in (1, xs - 1, 2) if d < xs]
    peers = peers[: xs - 1]

    def a_row(v, src, of, ssem, to):
        return send(src, gathered.at[v, of], ssem, a_recv.at[v, of], o, to)

    def a_wait(v, of):
        a_row(v, gathered.at[v, of], of, a_send.at[v, 0], twin).wait_recv()

    def a_own(v, to, core, i):
        return a_row(v, normed.at[2 * core + v], s, a_send.at[v, i], to)

    beside_all = [(beside - c + core, core) for core in range(2)]
    peers_all = [(peer + core, core) for peer in peers for core in range(2)]
    twin_all = [(twin, 1 - c)]

    def a_start(v, targets, first):
        for i, (to, core) in enumerate(targets):
            copy = a_own(v, to, core, first + i)
            copy.start()
            started.append(copy)

    started = []
    a_start(0, beside_all, 1)
    a_start(1, peers_all, 4)
    a_start(1, beside_all, 1)
    a_start(0, peers_all, 4)
    weights[0].start()
    a_start(1, twin_all, 3)
    a_start(0, twin_all, 3)
    for v in range(2):
        gathered[v, s] = normed[2 * c + v]
    for copy in weights[1:]:
        copy.start()
    round_signal(0)

    zero_rows = jnp.zeros((COLS, 9 * 128), F32)
    taps[0:COLS, :] = zero_rows
    taps[COLS + places :, :] = zero_rows
    step = places // 2
    col = lax.rem(lax.broadcasted_iota(jnp.int32, (step, 128), 0), COLS)

    def convolve(v):
        rows = gathered[v].reshape(places, chans)
        taps[COLS : COLS + places, :] = dot_trans(rows, wsp[...].reshape(9 * 128, chans))
        for part_of in range(2):
            base = part_of * step

            def column(j):
                total = None
                for tap in range(3):
                    start = base + tap * COLS
                    lane = (tap * 3 + j) * 128
                    term = taps[start : start + step, lane : lane + 128]
                    total = term if total is None else total + term
                return total

            left = jnp.where(col == 0, 0.0, pltpu.roll(column(0), 1, 0))
            right = jnp.where(col == COLS - 1, 0.0, pltpu.roll(column(2), step - 1, 0))
            total = left + column(1) + right
            total = total * (1.0 / (1.0 + jnp.exp(-total)))
            act[v, base : base + step] = total.astype(BF16)

    def forward(v, of, targets, first):
        a_wait(v, of)
        for i, to in enumerate(targets):
            copy = a_row(v, gathered.at[v, of], of, a_send.at[v, first + i], to)
            copy.start()
            started.append(copy)

    later = 4 + 2 * len(peers)
    for core in range(2):
        forward(0, beside - c + core, [peer + c for peer in peers], later + core * len(peers))
    for i, (of, _) in enumerate(peers_all):
        forward(1, of, [beside], later + i)

    round_wait(0)
    round_signal(1)
    loads[2].wait()
    weights[0].wait_recv()
    a_wait(1, twin)
    for of, _ in beside_all:
        a_wait(1, of)
    for peer in peers:
        for core in range(2):
            a_wait(1, peer + 2 - 4 * y + core)
    convolve(1)
    after = lax.rem(tau + 1, taus)
    edge_copy = send(
        act.at[1], edge, e_send.at[0], e_recv.at[0], after // 2, 2 * k + lax.rem(after, 2)
    )
    edge_copy.start()
    loads[3].wait()
    weights[1].wait_recv()
    round_wait(1)
    for i in range(2, last_round):
        round_signal(i)
        round_wait(i)
    if last_round > 1:
        round_signal(last_round)
    a_wait(0, twin)
    for of, _ in peers_all:
        a_wait(0, of)
    for peer in peers:
        for core in range(2):
            a_wait(0, peer + 2 - 4 * y + core)
    convolve(0)
    total = dot_plain(act[0], wtm[1].reshape(128, chans))
    total = total + dot_plain(act[1], wtm[2].reshape(128, chans))
    edge_copy.wait_recv()
    total = total + dot_plain(edge[...], wtm[0].reshape(128, chans))
    part[...] = total.reshape(spaces, 2, 8, chans).astype(BF16)

    def c_copy(half):
        def make(d):
            to = lax.rem(s + d, spaces)
            return send(
                part.at[to, half],
                part_in.at[half, k, c],
                c_send.at[half, d],
                c_recv.at[half, s],
                o,
                to,
            )

        return make

    def c_from(half):
        def make(d):
            frm = lax.rem(s + d, spaces)
            return send(
                part.at[0, half],
                part_in.at[half, frm // 2, lax.rem(frm, 2)],
                c_send.at[half, d],
                c_recv.at[half, frm],
                o,
                frm,
            )

        return make

    for half in range(2):
        each(spaces, c_copy(half), lambda copy: copy.start(), 1)
        sent.append((spaces, c_copy(half), 1))
        part_in[half, k, c] = part[s, half]

    if last_round > 1:
        round_wait(last_round)
    loads[4].wait()
    upper = lax.broadcasted_iota(jnp.int32, (8, chans), 0) < 4

    def d_target(q, to_x):
        to_o, to_c = worker(x, c, q)
        return to_o, to_x * 4 + y * 2 + to_c

    def d_copy(q, to_x):
        to_o, to_s = d_target(q, to_x)
        i = q * xs + to_x
        return send(d_out.at[q], d_in.at[o], d_send.at[i], d_recv.at[o], to_o, to_s)

    def is_here(to_o, to_s):
        return jnp.logical_and(to_o == o, to_s == s)

    for half in range(2):
        each(spaces, c_from(half), lambda copy: copy.wait_recv(), 1)
        if half == 1:
            pass
        total = jnp.sum(part_in[half].astype(F32), axis=0)
        rounded = total.astype(BF16)
        down[half] = rounded
        wide = rms(rounded.astype(F32), again[...])
        first, second = wide[0], wide[1]
        d_out[2 * half] = jnp.where(upper, first, pltpu.roll(second, 4, 0)).astype(BF16)
        d_out[2 * half + 1] = jnp.where(upper, pltpu.roll(first, 4, 0), second).astype(BF16)
        for q in (2 * half, 2 * half + 1):
            for to_x in range(xs):
                here = is_here(*d_target(q, to_x))

                @pl.when(here)
                def _(q=q):
                    pltpu.make_async_copy(d_out.at[q], d_in.at[o], d_recv.at[o]).start()

                @pl.when(jnp.logical_not(here))
                def _(q=q, to_x=to_x):
                    d_copy(q, to_x).start()

    weights[2].wait_recv()
    weights[3].wait_recv()
    for core in range(2):
        theirs = 2 - 2 * y + core
        send(
            qw_hbm, wqkv.at[:, theirs], y_send.at[0], y_recv.at[2 * core], across, beside
        ).wait_recv()
        send(
            ow_hbm, wout.at[theirs], y_send.at[0], y_recv.at[2 * core + 1], across, beside
        ).wait_recv()
    loads[5].wait()
    loads[6].wait()

    def d_from(i):
        return send(d_out.at[0], d_in.at[i], d_send.at[0], d_recv.at[i], i, served)

    each(orbits, d_from, lambda copy: copy.wait_recv())
    rows = d_in[...].astype(F32).reshape(pairs, chans).astype(BF16)
    qkv = dot_trans(rows, wqkv[...].reshape(3 * 4 * HD, chans))
    lane = lax.broadcasted_iota(jnp.int32, (pairs, 128), 1)
    left_place = lax.rem(lax.broadcasted_iota(jnp.int32, (pairs, pairs), 0), QUARTERS)
    right_place = lax.rem(lax.broadcasted_iota(jnp.int32, (pairs, pairs), 1), QUARTERS)
    same = left_place == right_place
    mixes = []
    for block in range(2):
        at = block * 128
        query = qkv[:, at : at + 128]
        key = qkv[:, 256 + at : 256 + at + 128].astype(BF16)
        value = qkv[:, 512 + at : 512 + at + 128].astype(BF16)
        heads = []
        for head in range(2):
            mine = (lane // HD) == head
            scores = dot_trans(jnp.where(mine, query, 0.0).astype(BF16), key) * (HD**-0.5)
            scores = jnp.where(same, scores, -jnp.inf)
            top = jnp.max(scores, axis=-1, keepdims=True)
            grown = jnp.exp(scores - top)
            probs = (grown / jnp.sum(grown, axis=-1, keepdims=True)).astype(BF16)
            heads.append(dot_plain(probs, value))
        mixes.append(jnp.where(lane < HD, heads[0], heads[1]).astype(BF16))
    wide_out = wout[...].reshape(4 * HD, chans)
    projected = dot_plain(mixes[0], wide_out[:128]) + dot_plain(mixes[1], wide_out[128:])
    proj[...] = projected.reshape(orbits, 8, chans).astype(BF16)

    def f_copy(i):
        return send(proj.at[i], f_in.at[x, wq], f_send.at[i], f_recv.at[4 * x + wq], i, served)

    def f_start(i, carry):
        here = is_here(i, served)

        @pl.when(here)
        def _():
            pltpu.make_async_copy(proj.at[i], f_in.at[x, wq], f_recv.at[4 * x + wq]).start()

        @pl.when(jnp.logical_not(here))
        def _():
            f_copy(i).start()

        return carry

    lax.fori_loop(0, orbits, f_start, 0)

    def f_from(i):
        return send(
            proj.at[0], f_in.at[i // 4, lax.rem(i, 4)], f_send.at[0], f_recv.at[i], o, twin
        )

    each(4 * xs, f_from, lambda copy: copy.wait_recv())
    for half in range(2):
        low = jnp.sum(f_in[:, 2 * half].astype(F32), axis=0)
        high = jnp.sum(f_in[:, 2 * half + 1].astype(F32), axis=0)
        first = jnp.where(upper, low, pltpu.roll(high, 4, 0))
        second = jnp.where(upper, pltpu.roll(low, 4, 0), high)
        bot_ref[0, half] = (down[half, 0].astype(F32) + first).astype(BF16)
        bot_ref[1, half] = (down[half, 1].astype(F32) + second).astype(BF16)

    for copy in weights + started:
        copy.wait_send()
    edge_copy.wait_send()
    for count, make, first in sent:
        each(count, make, lambda copy: copy.wait_send(), first)

    for q in range(4):
        for to_x in range(xs):

            @pl.when(jnp.logical_not(is_here(*d_target(q, to_x))))
            def _(q=q, to_x=to_x):
                d_copy(q, to_x).wait_send()

    def f_drain(i, carry):
        @pl.when(jnp.logical_not(is_here(i, served)))
        def _():
            f_copy(i).wait_send()

        return carry

    lax.fori_loop(0, orbits, f_drain, 0)


def body(latents, conv_gain, spatial_weight, temporal_weight, attn_gain, qkv_weight, out_weight):
    orbits, spaces = lax.axis_size("orbit"), lax.axis_size("space")
    chans = latents.shape[-1]
    chips, xs = spaces // 2, spaces // 4
    places = spaces * COLS
    vmem = pltpu.VMEM
    sem = pltpu.SemaphoreType.DMA
    bottom = pl.pallas_call(
        functools.partial(level_kernel, orbits, spaces),
        out_shape=jax.ShapeDtypeStruct((2, 2, 8, chans), BF16),
        in_specs=[pl.BlockSpec(memory_space=pltpu.HBM)] * 7,
        out_specs=pl.BlockSpec(memory_space=pltpu.VMEM),
        scratch_shapes=[
            vmem((4, 1, COLS, chans), BF16),
            vmem((1, chans), F32),
            vmem((1, chans), F32),
            vmem((9, 2, 64, chans), BF16),
            vmem((3, 2, 64, chans), BF16),
            vmem((3, 4, 64, chans), BF16),
            vmem((4, 64, chans), BF16),
            vmem((4, COLS, chans), BF16),
            vmem((2, spaces, COLS, chans), BF16),
            vmem((places + 2 * COLS, 9 * 128), F32),
            vmem((2, places, 128), BF16),
            vmem((places, 128), BF16),
            vmem((spaces, 2, 8, chans), BF16),
            vmem((2, chips, 2, 8, chans), BF16),
            vmem((2, 2, 8, chans), BF16),
            vmem((QUARTERS, 8, chans), BF16),
            vmem((orbits, 8, chans), BF16),
            vmem((orbits, 8, chans), BF16),
            vmem((xs, QUARTERS, 8, chans), BF16),
            sem((7,)),
            pltpu.SemaphoreType.REGULAR((4,)),
            sem((4,)),
            sem((4,)),
            sem((4,)),
            sem((4,)),
            sem((2, 4 + 2 * spaces)),
            sem((2, spaces)),
            sem((1,)),
            sem((1,)),
            sem((2, spaces)),
            sem((2, spaces)),
            sem((spaces,)),
            sem((orbits,)),
            sem((orbits,)),
            sem((spaces,)),
        ],
        compiler_params=pltpu.CompilerParams(
            collective_id=0, has_side_effects=True, vmem_limit_bytes=40 * 2**20
        ),
    )(
        *(
            pltpu.with_memory_space_constraint(array, pltpu.HBM)
            for array in (
                latents,
                conv_gain.reshape(1, chans),
                spatial_weight.reshape(9, 64, chans),
                temporal_weight,
                attn_gain.reshape(1, chans),
                qkv_weight,
                out_weight,
            )
        )
    )
    grown = jnp.repeat(bottom.reshape(2, COLS, chans), 2, axis=0)[:, None]
    return (latents.astype(F32) + grown.astype(F32)).astype(BF16)


def solution(mesh):
    return jax.shard_map(
        body,
        mesh=mesh,
        in_specs=(
            P("orbit", "space", None, None),
            P(),
            P(None, None, "space", None),
            P(None, "space", None),
            P(),
            P(None, "space", None),
            P("space", None),
        ),
        out_specs=P("orbit", "space", None, None),
        check_vma=False,
    )
```

```python
import functools

import jax
import jax.numpy as jnp
from jax import lax
from jax.experimental import pallas as pl
from jax.experimental.pallas import tpu as pltpu
from jax.sharding import PartitionSpec as P

HD = 64
COLS = 16
QUARTERS = 4
EPS = 1e-06
MESH = pl.DeviceIdType.MESH
F32 = jnp.float32
BF16 = jnp.bfloat16


def dot_trans(left, right):
    return lax.dot_general(left, right, (((1,), (1,)), ((), ())), preferred_element_type=F32)


def dot_plain(left, right):
    return jnp.dot(left, right, preferred_element_type=F32)


def rms(wide, gain):
    return wide * lax.rsqrt(jnp.mean(wide * wide, axis=-1, keepdims=True) + EPS) * gain


def level_kernel(
    orbits,
    spaces,
    lat_hbm,
    cgain_hbm,
    sw_hbm,
    tw_hbm,
    again_hbm,
    qw_hbm,
    ow_hbm,
    bot_ref,
    lat,
    cgain,
    again,
    wsp,
    wtm,
    wqkv,
    wout,
    normed,
    gathered,
    taps,
    act,
    edge,
    part,
    part_in,
    down,
    d_out,
    d_in,
    proj,
    f_in,
    local_sem,
    ring_sem,
    w_send,
    w_recv,
    y_send,
    y_recv,
    a_send,
    a_recv,
    e_send,
    e_recv,
    c_send,
    c_recv,
    d_send,
    d_recv,
    f_send,
    f_recv,
):
    xs = spaces // 4
    chips = spaces // 2
    taus = 2 * orbits
    chans = lat.shape[-1]
    places = spaces * COLS
    pairs = 8 * orbits
    o = lax.axis_index("orbit")
    s = lax.axis_index("space")
    c = lax.rem(s, 2)
    k = s // 2
    y = lax.rem(k, 2)
    x = s // 4
    slot = lax.rem(s, 4)
    tau = 2 * o + c
    twin = s + 1 - 2 * c
    beside = s + 2 - 4 * y
    across = lax.rem(o + orbits // 2, orbits)

    def worker(of_x, of_c, q):
        if xs == 1:
            return q, of_c
        return (of_x // 2) * 8 + of_c * 4 + q, lax.rem(of_x, 2)

    if xs == 1:
        wx, wc, wq = 0, c, o
    else:
        wx, wc, wq = (o // 8) * 2 + c, lax.rem(o, 8) // 4, lax.rem(o, 4)
    served = wx * 4 + y * 2 + wc

    def send(src, dst, ssem, rsem, to_o, to_s):
        return pltpu.make_async_remote_copy(
            src_ref=src,
            dst_ref=dst,
            send_sem=ssem,
            recv_sem=rsem,
            device_id=(to_o, to_s),
            device_id_type=MESH,
        )

    sent = []

    def each(count, make, what, first=0):
        def one(d, carry):
            what(make(d))
            return carry

        lax.fori_loop(first, count, one, 0)

    loads = [
        pltpu.make_async_copy(lat_hbm, lat, local_sem.at[0]),
        pltpu.make_async_copy(cgain_hbm, cgain, local_sem.at[1]),
        pltpu.make_async_copy(sw_hbm, wsp.at[:, c], local_sem.at[2]),
        pltpu.make_async_copy(tw_hbm, wtm.at[:, c], local_sem.at[3]),
        pltpu.make_async_copy(again_hbm, again, local_sem.at[4]),
        pltpu.make_async_copy(qw_hbm, wqkv.at[:, slot], local_sem.at[5]),
        pltpu.make_async_copy(ow_hbm, wout.at[slot], local_sem.at[6]),
    ]
    for load in loads:
        load.start()

    barrier = pltpu.get_barrier_semaphore()

    def signal(sem, to_o, to_s):
        pl.semaphore_signal(sem, inc=1, device_id=(to_o, to_s), device_id_type=MESH)

    def greet(d, carry):
        signal(barrier, o, lax.rem(s + d, spaces))
        return carry

    lax.fori_loop(1, spaces, greet, 0)
    signal(barrier, lax.rem(o + 1, orbits), s)
    signal(barrier, lax.rem(o + orbits - 1, orbits), s)
    signal(barrier, across, beside)

    rounds = []
    distance = 1
    while distance < orbits:
        rounds.append(distance)
        distance *= 2

    def round_signal(i):
        signal(ring_sem.at[i], lax.rem(o + rounds[i], orbits), s)
        if 2 * rounds[i] != orbits:
            signal(ring_sem.at[i], lax.rem(o + orbits - rounds[i], orbits), s)

    def round_wait(i):
        pl.semaphore_wait(ring_sem.at[i], 1 if 2 * rounds[i] == orbits else 2)

    def ring_step(i):
        if 0 < i <= len(rounds):
            round_wait(i - 1)
        if i < len(rounds):
            round_signal(i)

    loads[0].wait()
    loads[1].wait()
    row = rms(lat[...].astype(F32).reshape(4 * COLS, chans), cgain[...]).astype(BF16)
    normed[...] = row.reshape(4, COLS, chans)
    pl.semaphore_wait(barrier, spaces - 1 + 3)

    weights = [
        send(sw_hbm, wsp.at[:, c], w_send.at[0], w_recv.at[0], o, twin),
        send(tw_hbm, wtm.at[:, c], w_send.at[1], w_recv.at[1], o, twin),
        send(qw_hbm, wqkv.at[:, slot], w_send.at[2], w_recv.at[2], o, twin),
        send(ow_hbm, wout.at[slot], w_send.at[3], w_recv.at[3], o, twin),
    ]
    theirs = 2 - 2 * y + c
    weights.append(
        send(qw_hbm, wqkv.at[:, slot], y_send.at[0], y_recv.at[0], across, beside)
    )
    weights.append(
        send(ow_hbm, wout.at[slot], y_send.at[1], y_recv.at[1], across, beside)
    )
    passed = [
        send(wqkv.at[:, theirs], wqkv.at[:, theirs], y_send.at[2], y_recv.at[2], o, twin),
        send(wout.at[theirs], wout.at[theirs], y_send.at[3], y_recv.at[3], o, twin),
    ]

    def pass_on():
        weights[4].wait_recv()
        passed[0].start()
        weights[5].wait_recv()
        passed[1].start()

    peers = [lax.rem(x + d, xs) * 4 + 2 * y for d in (1, xs - 1, 2) if d < xs]
    peers = peers[: xs - 1]

    def a_row(v, src, of, ssem, to):
        return send(src, gathered.at[v, of], ssem, a_recv.at[v, of], o, to)

    def a_wait(v, of):
        a_row(v, gathered.at[v, of], of, a_send.at[v, 0], twin).wait_recv()

    def a_own(v, to, core, i):
        return a_row(v, normed.at[2 * core + v], s, a_send.at[v, i], to)

    beside_all = [(beside - c + core, core) for core in range(2)]
    peers_all = [(peer + core, core) for peer in peers for core in range(2)]
    twin_all = [(twin, 1 - c)]

    def a_start(v, targets, first):
        for i, (to, core) in enumerate(targets):
            copy = a_own(v, to, core, first + i)
            copy.start()
            started.append(copy)

    def forward(v, of, targets, first):
        a_wait(v, of)
        for i, to in enumerate(targets):
            copy = a_row(v, gathered.at[v, of], of, a_send.at[v, first + i], to)
            copy.start()
            started.append(copy)

    later = 4 + 2 * len(peers)

    def forward_x(v):
        forward(v, beside - c + 1, [peer + c for peer in peers], later)

    def forward_y(v):
        for i, peer in enumerate(peers):
            forward(v, peer, [beside], later + len(peers) + i)

    started = []
    a_start(1, beside_all, 1)
    a_start(1, peers_all, 4)
    weights[0].start()
    a_start(1, twin_all, 3)
    weights[4].start()
    weights[5].start()
    for v in range(2):
        gathered[v, s] = normed[2 * c + v]
    ring_step(0)

    zero_rows = jnp.zeros((COLS, 9 * 128), F32)
    taps[0:COLS, :] = zero_rows
    taps[COLS + places :, :] = zero_rows
    step = places // 2
    col = lax.rem(lax.broadcasted_iota(jnp.int32, (step, 128), 0), COLS)

    def convolve(v):
        rows = gathered[v].reshape(places, chans)
        taps[COLS : COLS + places, :] = dot_trans(rows, wsp[...].reshape(9 * 128, chans))
        for part_of in range(2):
            base = part_of * step

            def column(j):
                total = None
                for tap in range(3):
                    start = base + tap * COLS
                    lane = (tap * 3 + j) * 128
                    term = taps[start : start + step, lane : lane + 128]
                    total = term if total is None else total + term
                return total

            left = jnp.where(col == 0, 0.0, pltpu.roll(column(0), 1, 0))
            right = jnp.where(col == COLS - 1, 0.0, pltpu.roll(column(2), step - 1, 0))
            total = left + column(1) + right
            total = total * (1.0 / (1.0 + jnp.exp(-total)))
            act[v, base : base + step] = total.astype(BF16)

    a_start(0, beside_all, 1)
    a_start(0, peers_all, 4)
    a_start(0, twin_all, 3)
    for copy in weights[1:4]:
        copy.start()
    forward_x(1)
    ring_step(1)
    forward_y(1)
    forward_x(0)
    ring_step(2)
    forward_y(0)
    loads[2].wait()
    weights[0].wait_recv()
    a_wait(1, twin)
    a_wait(1, beside - c)
    for peer in peers:
        a_wait(1, peer + 1)
    for peer in peers:
        for core in range(2):
            a_wait(1, peer + 2 - 4 * y + core)
    convolve(1)
    after = lax.rem(tau + 1, taus)
    edge_copy = send(
        act.at[1], edge, e_send.at[0], e_recv.at[0], after // 2, 2 * k + lax.rem(after, 2)
    )
    edge_copy.start()
    loads[3].wait()
    weights[1].wait_recv()
    a_wait(0, twin)
    a_wait(0, beside - c)
    for peer in peers:
        a_wait(0, peer + 1)
    for peer in peers:
        for core in range(2):
            a_wait(0, peer + 2 - 4 * y + core)
    convolve(0)
    total = dot_plain(act[0], wtm[1].reshape(128, chans))
    total = total + dot_plain(act[1], wtm[2].reshape(128, chans))
    edge_copy.wait_recv()
    total = total + dot_plain(edge[...], wtm[0].reshape(128, chans))
    part[...] = total.reshape(spaces, 2, 8, chans).astype(BF16)

    def c_copy(half):
        def make(d):
            to = lax.rem(s + d, spaces)
            return send(
                part.at[to, half],
                part_in.at[half, k, c],
                c_send.at[half, d],
                c_recv.at[half, s],
                o,
                to,
            )

        return make

    def c_from(half):
        def make(d):
            frm = lax.rem(s + d, spaces)
            return send(
                part.at[0, half],
                part_in.at[half, frm // 2, lax.rem(frm, 2)],
                c_send.at[half, d],
                c_recv.at[half, frm],
                o,
                frm,
            )

        return make

    for half in range(2):
        each(spaces, c_copy(half), lambda copy: copy.start(), 1)
        sent.append((spaces, c_copy(half), 1))
        part_in[half, k, c] = part[s, half]

    ring_step(3)
    pass_on()
    ring_step(4)
    loads[4].wait()
    upper = lax.broadcasted_iota(jnp.int32, (8, chans), 0) < 4

    def d_target(q, to_x):
        to_o, to_c = worker(x, c, q)
        return to_o, to_x * 4 + y * 2 + to_c

    def d_copy(q, to_x):
        to_o, to_s = d_target(q, to_x)
        i = q * xs + to_x
        return send(d_out.at[q], d_in.at[o], d_send.at[i], d_recv.at[o], to_o, to_s)

    def is_here(to_o, to_s):
        return jnp.logical_and(to_o == o, to_s == s)

    for half in range(2):
        each(spaces, c_from(half), lambda copy: copy.wait_recv(), 1)
        if half == 1:
            pass
        total = jnp.sum(part_in[half].astype(F32), axis=0)
        rounded = total.astype(BF16)
        down[half] = rounded
        wide = rms(rounded.astype(F32), again[...])
        first, second = wide[0], wide[1]
        d_out[2 * half] = jnp.where(upper, first, pltpu.roll(second, 4, 0)).astype(BF16)
        d_out[2 * half + 1] = jnp.where(upper, pltpu.roll(first, 4, 0), second).astype(BF16)
        for q in (2 * half, 2 * half + 1):
            for to_x in range(xs):
                here = is_here(*d_target(q, to_x))

                @pl.when(here)
                def _(q=q):
                    pltpu.make_async_copy(d_out.at[q], d_in.at[o], d_recv.at[o]).start()

                @pl.when(jnp.logical_not(here))
                def _(q=q, to_x=to_x):
                    d_copy(q, to_x).start()

    weights[2].wait_recv()
    weights[3].wait_recv()
    for copy in passed:
        copy.wait_recv()
    loads[5].wait()
    loads[6].wait()

    def d_from(i):
        return send(d_out.at[0], d_in.at[i], d_send.at[0], d_recv.at[i], i, served)

    each(orbits, d_from, lambda copy: copy.wait_recv())
    rows = d_in[...].astype(F32).reshape(pairs, chans).astype(BF16)
    qkv = dot_trans(rows, wqkv[...].reshape(3 * 4 * HD, chans))
    lane = lax.broadcasted_iota(jnp.int32, (pairs, 128), 1)
    left_place = lax.rem(lax.broadcasted_iota(jnp.int32, (pairs, pairs), 0), QUARTERS)
    right_place = lax.rem(lax.broadcasted_iota(jnp.int32, (pairs, pairs), 1), QUARTERS)
    same = left_place == right_place
    mixes = []
    for block in range(2):
        at = block * 128
        query = qkv[:, at : at + 128]
        key = qkv[:, 256 + at : 256 + at + 128].astype(BF16)
        value = qkv[:, 512 + at : 512 + at + 128].astype(BF16)
        heads = []
        for head in range(2):
            mine = (lane // HD) == head
            scores = dot_trans(jnp.where(mine, query, 0.0).astype(BF16), key) * (HD**-0.5)
            scores = jnp.where(same, scores, -jnp.inf)
            top = jnp.max(scores, axis=-1, keepdims=True)
            grown = jnp.exp(scores - top)
            probs = (grown / jnp.sum(grown, axis=-1, keepdims=True)).astype(BF16)
            heads.append(dot_plain(probs, value))
        mixes.append(jnp.where(lane < HD, heads[0], heads[1]).astype(BF16))
    wide_out = wout[...].reshape(4 * HD, chans)
    projected = dot_plain(mixes[0], wide_out[:128]) + dot_plain(mixes[1], wide_out[128:])
    proj[...] = projected.reshape(orbits, 8, chans).astype(BF16)

    def f_copy(i):
        return send(proj.at[i], f_in.at[x, wq], f_send.at[i], f_recv.at[4 * x + wq], i, served)

    def f_start(i, carry):
        here = is_here(i, served)

        @pl.when(here)
        def _():
            pltpu.make_async_copy(proj.at[i], f_in.at[x, wq], f_recv.at[4 * x + wq]).start()

        @pl.when(jnp.logical_not(here))
        def _():
            f_copy(i).start()

        return carry

    lax.fori_loop(0, orbits, f_start, 0)

    def f_from(i):
        return send(
            proj.at[0], f_in.at[i // 4, lax.rem(i, 4)], f_send.at[0], f_recv.at[i], o, twin
        )

    each(4 * xs, f_from, lambda copy: copy.wait_recv())
    for half in range(2):
        low = jnp.sum(f_in[:, 2 * half].astype(F32), axis=0)
        high = jnp.sum(f_in[:, 2 * half + 1].astype(F32), axis=0)
        first = jnp.where(upper, low, pltpu.roll(high, 4, 0))
        second = jnp.where(upper, pltpu.roll(low, 4, 0), high)
        bot_ref[0, half] = (down[half, 0].astype(F32) + first).astype(BF16)
        bot_ref[1, half] = (down[half, 1].astype(F32) + second).astype(BF16)

    for copy in weights + passed + started:
        copy.wait_send()
    edge_copy.wait_send()
    for count, make, first in sent:
        each(count, make, lambda copy: copy.wait_send(), first)

    for q in range(4):
        for to_x in range(xs):

            @pl.when(jnp.logical_not(is_here(*d_target(q, to_x))))
            def _(q=q, to_x=to_x):
                d_copy(q, to_x).wait_send()

    def f_drain(i, carry):
        @pl.when(jnp.logical_not(is_here(i, served)))
        def _():
            f_copy(i).wait_send()

        return carry

    lax.fori_loop(0, orbits, f_drain, 0)


def body(latents, conv_gain, spatial_weight, temporal_weight, attn_gain, qkv_weight, out_weight):
    orbits, spaces = lax.axis_size("orbit"), lax.axis_size("space")
    chans = latents.shape[-1]
    chips, xs = spaces // 2, spaces // 4
    places = spaces * COLS
    vmem = pltpu.VMEM
    sem = pltpu.SemaphoreType.DMA
    bottom = pl.pallas_call(
        functools.partial(level_kernel, orbits, spaces),
        out_shape=jax.ShapeDtypeStruct((2, 2, 8, chans), BF16),
        in_specs=[pl.BlockSpec(memory_space=pltpu.HBM)] * 7,
        out_specs=pl.BlockSpec(memory_space=pltpu.VMEM),
        scratch_shapes=[
            vmem((4, 1, COLS, chans), BF16),
            vmem((1, chans), F32),
            vmem((1, chans), F32),
            vmem((9, 2, 64, chans), BF16),
            vmem((3, 2, 64, chans), BF16),
            vmem((3, 4, 64, chans), BF16),
            vmem((4, 64, chans), BF16),
            vmem((4, COLS, chans), BF16),
            vmem((2, spaces, COLS, chans), BF16),
            vmem((places + 2 * COLS, 9 * 128), F32),
            vmem((2, places, 128), BF16),
            vmem((places, 128), BF16),
            vmem((spaces, 2, 8, chans), BF16),
            vmem((2, chips, 2, 8, chans), BF16),
            vmem((2, 2, 8, chans), BF16),
            vmem((QUARTERS, 8, chans), BF16),
            vmem((orbits, 8, chans), BF16),
            vmem((orbits, 8, chans), BF16),
            vmem((xs, QUARTERS, 8, chans), BF16),
            sem((7,)),
            pltpu.SemaphoreType.REGULAR((4,)),
            sem((4,)),
            sem((4,)),
            sem((4,)),
            sem((4,)),
            sem((2, 4 + 2 * spaces)),
            sem((2, spaces)),
            sem((1,)),
            sem((1,)),
            sem((2, spaces)),
            sem((2, spaces)),
            sem((spaces,)),
            sem((orbits,)),
            sem((orbits,)),
            sem((spaces,)),
        ],
        compiler_params=pltpu.CompilerParams(
            collective_id=0, has_side_effects=True, vmem_limit_bytes=40 * 2**20
        ),
    )(
        *(
            pltpu.with_memory_space_constraint(array, pltpu.HBM)
            for array in (
                latents,
                conv_gain.reshape(1, chans),
                spatial_weight.reshape(9, 64, chans),
                temporal_weight,
                attn_gain.reshape(1, chans),
                qkv_weight,
                out_weight,
            )
        )
    )
    grown = jnp.repeat(bottom.reshape(2, COLS, chans), 2, axis=0)[:, None]
    return (latents.astype(F32) + grown.astype(F32)).astype(BF16)


def solution(mesh):
    return jax.shard_map(
        body,
        mesh=mesh,
        in_specs=(
            P("orbit", "space", None, None),
            P(),
            P(None, None, "space", None),
            P(None, "space", None),
            P(),
            P(None, "space", None),
            P("space", None),
        ),
        out_specs=P("orbit", "space", None, None),
        check_vma=False,
    )
```

```python
import functools

import jax
import jax.numpy as jnp
from jax import lax
from jax.experimental import pallas as pl
from jax.experimental.pallas import tpu as pltpu
from jax.sharding import PartitionSpec as P

HD = 64
COLS = 16
QUARTERS = 4
EPS = 1e-06
MESH = pl.DeviceIdType.MESH
F32 = jnp.float32
BF16 = jnp.bfloat16


def dot_trans(left, right):
    return lax.dot_general(left, right, (((1,), (1,)), ((), ())), preferred_element_type=F32)


def dot_plain(left, right):
    return jnp.dot(left, right, preferred_element_type=F32)


def rms(wide, gain):
    return wide * lax.rsqrt(jnp.mean(wide * wide, axis=-1, keepdims=True) + EPS) * gain


def level_kernel(
    orbits,
    spaces,
    lat_hbm,
    cgain_hbm,
    sw_hbm,
    tw_hbm,
    again_hbm,
    qw_hbm,
    ow_hbm,
    bot_ref,
    lat,
    cgain,
    again,
    wsp,
    wtm,
    wqkv,
    wout,
    wqkv_turned,
    normed,
    gathered,
    taps,
    act,
    edge,
    part,
    part_in,
    down,
    d_out,
    d_in,
    proj,
    f_in,
    local_sem,
    ring_sem,
    w_send,
    w_recv,
    y_send,
    y_recv,
    a_send,
    a_recv,
    e_send,
    e_recv,
    c_send,
    c_recv,
    d_send,
    d_recv,
    f_send,
    f_recv,
):
    xs = spaces // 4
    chips = spaces // 2
    taus = 2 * orbits
    chans = lat.shape[-1]
    places = spaces * COLS
    pairs = 8 * orbits
    o = lax.axis_index("orbit")
    s = lax.axis_index("space")
    c = lax.rem(s, 2)
    k = s // 2
    y = lax.rem(k, 2)
    x = s // 4
    slot = lax.rem(s, 4)
    tau = 2 * o + c
    twin = s + 1 - 2 * c
    beside = s + 2 - 4 * y
    across = lax.rem(o + orbits // 2, orbits)

    def worker(of_x, of_c, q):
        if xs == 1:
            return q, of_c
        return (of_x // 2) * 8 + of_c * 4 + q, lax.rem(of_x, 2)

    if xs == 1:
        wx, wc, wq = 0, c, o
    else:
        wx, wc, wq = (o // 8) * 2 + c, lax.rem(o, 8) // 4, lax.rem(o, 4)
    served = wx * 4 + y * 2 + wc

    def send(src, dst, ssem, rsem, to_o, to_s):
        return pltpu.make_async_remote_copy(
            src_ref=src,
            dst_ref=dst,
            send_sem=ssem,
            recv_sem=rsem,
            device_id=(to_o, to_s),
            device_id_type=MESH,
        )

    sent = []

    def each(count, make, what, first=0):
        def one(d, carry):
            what(make(d))
            return carry

        lax.fori_loop(first, count, one, 0)

    loads = [
        pltpu.make_async_copy(lat_hbm, lat, local_sem.at[0]),
        pltpu.make_async_copy(cgain_hbm, cgain, local_sem.at[1]),
        pltpu.make_async_copy(sw_hbm, wsp.at[:, c], local_sem.at[2]),
        pltpu.make_async_copy(tw_hbm, wtm.at[:, c], local_sem.at[3]),
        pltpu.make_async_copy(again_hbm, again, local_sem.at[4]),
        pltpu.make_async_copy(qw_hbm, wqkv.at[:, slot], local_sem.at[5]),
        pltpu.make_async_copy(ow_hbm, wout.at[slot], local_sem.at[6]),
    ]
    for load in loads:
        load.start()

    barrier = pltpu.get_barrier_semaphore()

    def signal(sem, to_o, to_s):
        pl.semaphore_signal(sem, inc=1, device_id=(to_o, to_s), device_id_type=MESH)

    peers = [lax.rem(x + d, xs) * 4 + 2 * y for d in (1, xs - 1, 2) if d < xs]
    peers = peers[: xs - 1]
    beside_all = [(beside - c + core, core) for core in range(2)]
    peers_all = [(peer + core, core) for peer in peers for core in range(2)]
    twin_all = [(twin, 1 - c)]
    for to, _ in peers_all + beside_all + twin_all:
        signal(barrier, o, to)
    signal(barrier, lax.rem(o + 1, orbits), s)
    signal(barrier, lax.rem(o + orbits - 1, orbits), s)
    signal(barrier, across, beside)

    rounds = []
    distance = 1
    while distance < orbits:
        rounds.append(distance)
        distance *= 2

    def round_signal(i):
        signal(ring_sem.at[i], lax.rem(o + rounds[i], orbits), s)
        if 2 * rounds[i] != orbits:
            signal(ring_sem.at[i], lax.rem(o + orbits - rounds[i], orbits), s)

    def round_wait(i):
        pl.semaphore_wait(ring_sem.at[i], 1 if 2 * rounds[i] == orbits else 2)

    def ring_step(i):
        if 0 < i <= len(rounds):
            round_wait(i - 1)
        if i < len(rounds):
            round_signal(i)

    loads[0].wait()
    loads[1].wait()
    row = rms(lat[...].astype(F32).reshape(4 * COLS, chans), cgain[...]).astype(BF16)
    normed[...] = row.reshape(4, COLS, chans)
    pl.semaphore_wait(barrier, 2 * len(peers) + 3 + 3)

    weights = [
        send(sw_hbm, wsp.at[:, c], w_send.at[0], w_recv.at[0], o, twin),
        send(tw_hbm, wtm.at[:, c], w_send.at[1], w_recv.at[1], o, twin),
        send(qw_hbm, wqkv.at[:, slot], w_send.at[2], w_recv.at[2], o, twin),
        send(ow_hbm, wout.at[slot], w_send.at[3], w_recv.at[3], o, twin),
    ]
    theirs = 2 - 2 * y + c
    weights.append(
        send(qw_hbm, wqkv.at[:, slot], y_send.at[0], y_recv.at[0], across, beside)
    )
    weights.append(
        send(ow_hbm, wout.at[slot], y_send.at[1], y_recv.at[1], across, beside)
    )
    passed = [
        send(wqkv.at[:, theirs], wqkv.at[:, theirs], y_send.at[2], y_recv.at[2], o, twin),
        send(wout.at[theirs], wout.at[theirs], y_send.at[3], y_recv.at[3], o, twin),
    ]

    def pass_on():
        weights[4].wait_recv()
        passed[0].start()
        weights[5].wait_recv()
        passed[1].start()

    def a_row(v, src, of, ssem, to):
        return send(src, gathered.at[v, of], ssem, a_recv.at[v, of], o, to)

    def a_wait(v, of):
        a_row(v, gathered.at[v, of], of, a_send.at[v, 0], twin).wait_recv()

    def a_own(v, to, core, i):
        return a_row(v, normed.at[2 * core + v], s, a_send.at[v, i], to)

    def a_start(v, targets, first):
        for i, (to, core) in enumerate(targets):
            copy = a_own(v, to, core, first + i)
            copy.start()
            started.append(copy)

    def forward(v, of, targets, first):
        a_wait(v, of)
        for i, to in enumerate(targets):
            copy = a_row(v, gathered.at[v, of], of, a_send.at[v, first + i], to)
            copy.start()
            started.append(copy)

    later = 4 + 2 * len(peers)

    def forward_x(v):
        forward(v, beside - c + 1, [peer + c for peer in peers], later)

    def forward_y(v):
        for i, peer in enumerate(peers):
            forward(v, peer, [beside], later + len(peers) + i)

    started = []
    a_start(1, beside_all, 1)
    a_start(1, peers_all, 4)
    weights[0].start()
    a_start(1, twin_all, 3)
    weights[4].start()
    weights[5].start()
    for v in range(2):
        gathered[v, s] = normed[2 * c + v]
    ring_step(0)

    zero_rows = jnp.zeros((COLS, 9 * 128), F32)
    taps[0:COLS, :] = zero_rows
    taps[COLS + places :, :] = zero_rows
    step = places // 2
    col = lax.rem(lax.broadcasted_iota(jnp.int32, (step, 128), 0), COLS)

    def convolve(v):
        rows = gathered[v].reshape(places, chans)
        taps[COLS : COLS + places, :] = dot_trans(rows, wsp[...].reshape(9 * 128, chans))
        for part_of in range(2):
            base = part_of * step

            def column(j):
                total = None
                for tap in range(3):
                    start = base + tap * COLS
                    lane = (tap * 3 + j) * 128
                    term = taps[start : start + step, lane : lane + 128]
                    total = term if total is None else total + term
                return total

            left = jnp.where(col == 0, 0.0, pltpu.roll(column(0), 1, 0))
            right = jnp.where(col == COLS - 1, 0.0, pltpu.roll(column(2), step - 1, 0))
            total = left + column(1) + right
            total = total * (1.0 / (1.0 + jnp.exp(-total)))
            act[v, base : base + step] = total.astype(BF16)

    a_start(0, beside_all, 1)
    a_start(0, peers_all, 4)
    a_start(0, twin_all, 3)
    for copy in weights[1:4]:
        copy.start()
    forward_x(1)
    ring_step(1)
    forward_y(1)
    forward_x(0)
    ring_step(2)
    forward_y(0)
    loads[2].wait()
    weights[0].wait_recv()
    a_wait(1, twin)
    a_wait(1, beside - c)
    for peer in peers:
        a_wait(1, peer + 1)
    for peer in peers:
        for core in range(2):
            a_wait(1, peer + 2 - 4 * y + core)
    convolve(1)
    after = lax.rem(tau + 1, taus)
    edge_copy = send(
        act.at[1], edge, e_send.at[0], e_recv.at[0], after // 2, 2 * k + lax.rem(after, 2)
    )
    edge_copy.start()
    loads[3].wait()
    weights[1].wait_recv()
    a_wait(0, twin)
    a_wait(0, beside - c)
    for peer in peers:
        a_wait(0, peer + 1)
    for peer in peers:
        for core in range(2):
            a_wait(0, peer + 2 - 4 * y + core)
    convolve(0)
    total = dot_plain(act[0], wtm[1].reshape(128, chans))
    total = total + dot_plain(act[1], wtm[2].reshape(128, chans))
    edge_copy.wait_recv()
    total = total + dot_plain(edge[...], wtm[0].reshape(128, chans))
    part[...] = total.reshape(spaces, 2, 8, chans).astype(BF16)

    def c_copy(half):
        def make(d):
            to = lax.rem(s + d, spaces)
            return send(
                part.at[to, half],
                part_in.at[half, k, c],
                c_send.at[half, d],
                c_recv.at[half, s],
                o,
                to,
            )

        return make

    def c_from(half):
        def make(d):
            frm = lax.rem(s + d, spaces)
            return send(
                part.at[0, half],
                part_in.at[half, frm // 2, lax.rem(frm, 2)],
                c_send.at[half, d],
                c_recv.at[half, frm],
                o,
                frm,
            )

        return make

    for half in range(2):
        each(spaces, c_copy(half), lambda copy: copy.start(), 1)
        sent.append((spaces, c_copy(half), 1))
        part_in[half, k, c] = part[s, half]

    ring_step(3)
    pass_on()
    weights[2].wait_recv()
    weights[3].wait_recv()
    loads[5].wait()
    loads[6].wait()
    for copy in passed:
        copy.wait_recv()
    wqkv_turned[...] = wqkv[...].reshape(3 * 4 * HD, chans).T
    ring_step(4)
    loads[4].wait()
    upper = lax.broadcasted_iota(jnp.int32, (8, chans), 0) < 4

    def d_target(q, to_x):
        to_o, to_c = worker(x, c, q)
        return to_o, to_x * 4 + y * 2 + to_c

    def d_copy(q, to_x):
        to_o, to_s = d_target(q, to_x)
        i = q * xs + to_x
        return send(d_out.at[q], d_in.at[o], d_send.at[i], d_recv.at[o], to_o, to_s)

    def is_here(to_o, to_s):
        return jnp.logical_and(to_o == o, to_s == s)

    for half in range(2):
        each(spaces, c_from(half), lambda copy: copy.wait_recv(), 1)
        if half == 1:
            pass
        total = jnp.sum(part_in[half].astype(F32), axis=0)
        rounded = total.astype(BF16)
        down[half] = rounded
        wide = rms(rounded.astype(F32), again[...])
        first, second = wide[0], wide[1]
        d_out[2 * half] = jnp.where(upper, first, pltpu.roll(second, 4, 0)).astype(BF16)
        d_out[2 * half + 1] = jnp.where(upper, pltpu.roll(first, 4, 0), second).astype(BF16)
        for q in (2 * half, 2 * half + 1):
            for d in (2, 1, 3, 0):
                if d >= xs:
                    continue
                to_x = lax.rem(x + d, xs)
                here = is_here(*d_target(q, to_x))

                @pl.when(here)
                def _(q=q):
                    pltpu.make_async_copy(d_out.at[q], d_in.at[o], d_recv.at[o]).start()

                @pl.when(jnp.logical_not(here))
                def _(q=q, to_x=to_x):
                    d_copy(q, to_x).start()


    def d_from(i):
        return send(d_out.at[0], d_in.at[i], d_send.at[0], d_recv.at[i], i, served)

    each(orbits, d_from, lambda copy: copy.wait_recv())
    rows = d_in[...].astype(F32).reshape(pairs, chans).astype(BF16)
    qkv = dot_plain(rows, wqkv_turned[...])
    head_of = lax.broadcasted_iota(jnp.int32, (pairs, 4 * HD), 1) // HD
    query = qkv[:, : 4 * HD]
    key = qkv[:, 4 * HD : 8 * HD].astype(BF16)
    value = qkv[:, 8 * HD :].astype(BF16)
    apart = [jnp.where(head_of == head, query, 0.0).astype(BF16) for head in range(4)]
    scores = dot_trans(jnp.concatenate(apart, axis=0), key) * (HD**-0.5)
    left_place = lax.rem(lax.broadcasted_iota(jnp.int32, scores.shape, 0), QUARTERS)
    right_place = lax.rem(lax.broadcasted_iota(jnp.int32, scores.shape, 1), QUARTERS)
    scores = jnp.where(left_place == right_place, scores, -jnp.inf)
    grown = jnp.exp(scores - jnp.max(scores, axis=-1, keepdims=True))
    probs = (grown * (1.0 / jnp.sum(grown, axis=-1, keepdims=True))).astype(BF16)
    every = dot_plain(probs, value)
    mixed = every[:pairs]
    for head in range(1, 4):
        mixed = jnp.where(head_of == head, every[head * pairs : (head + 1) * pairs], mixed)
    projected = dot_plain(mixed.astype(BF16), wout[...].reshape(4 * HD, chans))
    proj[...] = projected.reshape(orbits, 8, chans).astype(BF16)

    def f_copy(i):
        return send(proj.at[i], f_in.at[x, wq], f_send.at[i], f_recv.at[4 * x + wq], i, served)

    def f_start(i, carry):
        here = is_here(i, served)

        @pl.when(here)
        def _():
            pltpu.make_async_copy(proj.at[i], f_in.at[x, wq], f_recv.at[4 * x + wq]).start()

        @pl.when(jnp.logical_not(here))
        def _():
            f_copy(i).start()

        return carry

    lax.fori_loop(0, orbits, f_start, 0)

    def f_from(i):
        return send(
            proj.at[0], f_in.at[i // 4, lax.rem(i, 4)], f_send.at[0], f_recv.at[i], o, twin
        )

    each(4 * xs, f_from, lambda copy: copy.wait_recv())
    for half in range(2):
        low = jnp.sum(f_in[:, 2 * half].astype(F32), axis=0)
        high = jnp.sum(f_in[:, 2 * half + 1].astype(F32), axis=0)
        first = jnp.where(upper, low, pltpu.roll(high, 4, 0))
        second = jnp.where(upper, pltpu.roll(low, 4, 0), high)
        bot_ref[0, half] = (down[half, 0].astype(F32) + first).astype(BF16)
        bot_ref[1, half] = (down[half, 1].astype(F32) + second).astype(BF16)

    for copy in weights + passed + started:
        copy.wait_send()
    edge_copy.wait_send()
    for count, make, first in sent:
        each(count, make, lambda copy: copy.wait_send(), first)

    for q in range(4):
        for to_x in range(xs):

            @pl.when(jnp.logical_not(is_here(*d_target(q, to_x))))
            def _(q=q, to_x=to_x):
                d_copy(q, to_x).wait_send()

    def f_drain(i, carry):
        @pl.when(jnp.logical_not(is_here(i, served)))
        def _():
            f_copy(i).wait_send()

        return carry

    lax.fori_loop(0, orbits, f_drain, 0)


def body(latents, conv_gain, spatial_weight, temporal_weight, attn_gain, qkv_weight, out_weight):
    orbits, spaces = lax.axis_size("orbit"), lax.axis_size("space")
    chans = latents.shape[-1]
    chips, xs = spaces // 2, spaces // 4
    places = spaces * COLS
    vmem = pltpu.VMEM
    sem = pltpu.SemaphoreType.DMA
    bottom = pl.pallas_call(
        functools.partial(level_kernel, orbits, spaces),
        out_shape=jax.ShapeDtypeStruct((2, 2, 8, chans), BF16),
        in_specs=[pl.BlockSpec(memory_space=pltpu.HBM)] * 7,
        out_specs=pl.BlockSpec(memory_space=pltpu.VMEM),
        scratch_shapes=[
            vmem((4, 1, COLS, chans), BF16),
            vmem((1, chans), F32),
            vmem((1, chans), F32),
            vmem((9, 2, 64, chans), BF16),
            vmem((3, 2, 64, chans), BF16),
            vmem((3, 4, 64, chans), BF16),
            vmem((4, 64, chans), BF16),
            vmem((chans, 3 * 4 * HD), BF16),
            vmem((4, COLS, chans), BF16),
            vmem((2, spaces, COLS, chans), BF16),
            vmem((places + 2 * COLS, 9 * 128), F32),
            vmem((2, places, 128), BF16),
            vmem((places, 128), BF16),
            vmem((spaces, 2, 8, chans), BF16),
            vmem((2, chips, 2, 8, chans), BF16),
            vmem((2, 2, 8, chans), BF16),
            vmem((QUARTERS, 8, chans), BF16),
            vmem((orbits, 8, chans), BF16),
            vmem((orbits, 8, chans), BF16),
            vmem((xs, QUARTERS, 8, chans), BF16),
            sem((7,)),
            pltpu.SemaphoreType.REGULAR((4,)),
            sem((4,)),
            sem((4,)),
            sem((4,)),
            sem((4,)),
            sem((2, 4 + 2 * spaces)),
            sem((2, spaces)),
            sem((1,)),
            sem((1,)),
            sem((2, spaces)),
            sem((2, spaces)),
            sem((spaces,)),
            sem((orbits,)),
            sem((orbits,)),
            sem((spaces,)),
        ],
        compiler_params=pltpu.CompilerParams(
            collective_id=0, has_side_effects=True, vmem_limit_bytes=40 * 2**20
        ),
    )(
        *(
            pltpu.with_memory_space_constraint(array, pltpu.HBM)
            for array in (
                latents,
                conv_gain.reshape(1, chans),
                spatial_weight.reshape(9, 64, chans),
                temporal_weight,
                attn_gain.reshape(1, chans),
                qkv_weight,
                out_weight,
            )
        )
    )
    grown = jnp.repeat(bottom.reshape(2, COLS, chans), 2, axis=0)[:, None]
    return (latents.astype(F32) + grown.astype(F32)).astype(BF16)


def solution(mesh):
    return jax.shard_map(
        body,
        mesh=mesh,
        in_specs=(
            P("orbit", "space", None, None),
            P(),
            P(None, None, "space", None),
            P(None, "space", None),
            P(),
            P(None, "space", None),
            P("space", None),
        ),
        out_specs=P("orbit", "space", None, None),
        check_vma=False,
    )
```

```python
import functools

import jax
import jax.numpy as jnp
from jax import lax
from jax.experimental import pallas as pl
from jax.experimental.pallas import tpu as pltpu
from jax.sharding import PartitionSpec as P

HD = 64
COLS = 16
QUARTERS = 4
EPS = 1e-06
MESH = pl.DeviceIdType.MESH
F32 = jnp.float32
BF16 = jnp.bfloat16


def dot_trans(left, right):
    return lax.dot_general(left, right, (((1,), (1,)), ((), ())), preferred_element_type=F32)


def dot_plain(left, right):
    return jnp.dot(left, right, preferred_element_type=F32)


def rms(wide, gain):
    return wide * lax.rsqrt(jnp.mean(wide * wide, axis=-1, keepdims=True) + EPS) * gain


def level_kernel(
    orbits,
    spaces,
    lat_hbm,
    cgain_hbm,
    sw_hbm,
    tw_hbm,
    again_hbm,
    qw_hbm,
    ow_hbm,
    bot_ref,
    lat,
    cgain,
    again,
    wsp,
    wtm,
    wqkv,
    wout,
    wqkv_turned,
    normed,
    gathered,
    taps,
    act,
    edge,
    part,
    part_in,
    down,
    d_out,
    d_in,
    proj,
    f_in,
    local_sem,
    ring_sem,
    w_send,
    w_recv,
    y_send,
    y_recv,
    a_send,
    a_recv,
    e_send,
    e_recv,
    c_send,
    c_recv,
    d_send,
    d_recv,
    f_send,
    f_recv,
):
    xs = spaces // 4
    chips = spaces // 2
    taus = 2 * orbits
    chans = lat.shape[-1]
    places = spaces * COLS
    pairs = 8 * orbits
    o = lax.axis_index("orbit")
    s = lax.axis_index("space")
    c = lax.rem(s, 2)
    k = s // 2
    y = lax.rem(k, 2)
    x = s // 4
    slot = lax.rem(s, 4)
    tau = 2 * o + c
    twin = s + 1 - 2 * c
    beside = s + 2 - 4 * y
    across = lax.rem(o + orbits // 2, orbits)

    def worker(of_x, of_c, q):
        if xs == 1:
            return q, of_c
        return (of_x // 2) * 8 + of_c * 4 + q, lax.rem(of_x, 2)

    if xs == 1:
        wx, wc, wq = 0, c, o
    else:
        wx, wc, wq = (o // 8) * 2 + c, lax.rem(o, 8) // 4, lax.rem(o, 4)
    served = wx * 4 + y * 2 + wc

    def send(src, dst, ssem, rsem, to_o, to_s):
        return pltpu.make_async_remote_copy(
            src_ref=src,
            dst_ref=dst,
            send_sem=ssem,
            recv_sem=rsem,
            device_id=(to_o, to_s),
            device_id_type=MESH,
        )

    sent = []

    def each(count, make, what, first=0):
        def one(d, carry):
            what(make(d))
            return carry

        lax.fori_loop(first, count, one, 0)

    loads = [
        pltpu.make_async_copy(lat_hbm, lat, local_sem.at[0]),
        pltpu.make_async_copy(cgain_hbm, cgain, local_sem.at[1]),
        pltpu.make_async_copy(sw_hbm, wsp.at[:, c], local_sem.at[2]),
        pltpu.make_async_copy(tw_hbm, wtm.at[:, c], local_sem.at[3]),
        pltpu.make_async_copy(again_hbm, again, local_sem.at[4]),
        pltpu.make_async_copy(qw_hbm, wqkv.at[:, slot], local_sem.at[5]),
        pltpu.make_async_copy(ow_hbm, wout.at[slot], local_sem.at[6]),
    ]
    for load in loads:
        load.start()

    barrier = pltpu.get_barrier_semaphore()

    def signal(sem, to_o, to_s):
        pl.semaphore_signal(sem, inc=1, device_id=(to_o, to_s), device_id_type=MESH)

    peers = [lax.rem(x + d, xs) * 4 + 2 * y for d in (1, xs - 1, 2) if d < xs]
    peers = peers[: xs - 1]
    beside_all = [(beside - c + core, core) for core in range(2)]
    peers_all = [(peer + core, core) for peer in peers for core in range(2)]
    twin_all = [(twin, 1 - c)]
    for to, _ in peers_all + beside_all + twin_all:
        signal(barrier, o, to)
    signal(barrier, lax.rem(o + 1, orbits), s)
    signal(barrier, lax.rem(o + orbits - 1, orbits), s)
    signal(barrier, across, beside)

    rounds = []
    distance = 1
    while distance < orbits:
        rounds.append(distance)
        distance *= 2

    def round_signal(i):
        signal(ring_sem.at[i], lax.rem(o + rounds[i], orbits), s)
        if 2 * rounds[i] != orbits:
            signal(ring_sem.at[i], lax.rem(o + orbits - rounds[i], orbits), s)

    def round_wait(i):
        pl.semaphore_wait(ring_sem.at[i], 1 if 2 * rounds[i] == orbits else 2)

    def ring_step(i):
        if 0 < i <= len(rounds):
            round_wait(i - 1)
        if i < len(rounds):
            round_signal(i)

    loads[0].wait()
    loads[1].wait()
    row = rms(lat[...].astype(F32).reshape(4 * COLS, chans), cgain[...]).astype(BF16)
    normed[...] = row.reshape(4, COLS, chans)
    pl.semaphore_wait(barrier, 2 * len(peers) + 3 + 3)

    weights = [
        send(sw_hbm, wsp.at[:, c], w_send.at[0], w_recv.at[0], o, twin),
        send(tw_hbm, wtm.at[:, c], w_send.at[1], w_recv.at[1], o, twin),
        send(qw_hbm, wqkv.at[:, slot], w_send.at[2], w_recv.at[2], o, twin),
        send(ow_hbm, wout.at[slot], w_send.at[3], w_recv.at[3], o, twin),
    ]
    theirs = 2 - 2 * y + c
    weights.append(
        send(qw_hbm, wqkv.at[:, slot], y_send.at[0], y_recv.at[0], across, beside)
    )
    weights.append(
        send(ow_hbm, wout.at[slot], y_send.at[1], y_recv.at[1], across, beside)
    )
    passed = [
        send(wqkv.at[:, theirs], wqkv.at[:, theirs], y_send.at[2], y_recv.at[2], o, twin),
        send(wout.at[theirs], wout.at[theirs], y_send.at[3], y_recv.at[3], o, twin),
    ]

    def pass_on():
        weights[4].wait_recv()
        passed[0].start()
        weights[5].wait_recv()
        passed[1].start()

    def a_row(v, src, of, ssem, to):
        return send(src, gathered.at[v, of], ssem, a_recv.at[v, of], o, to)

    def a_wait(v, of):
        a_row(v, gathered.at[v, of], of, a_send.at[v, 0], twin).wait_recv()

    def a_own(v, to, core, i):
        return a_row(v, normed.at[2 * core + v], s, a_send.at[v, i], to)

    def a_start(v, targets, first):
        for i, (to, core) in enumerate(targets):
            copy = a_own(v, to, core, first + i)
            copy.start()
            started.append(copy)

    def forward(v, of, targets, first):
        a_wait(v, of)
        for i, to in enumerate(targets):
            copy = a_row(v, gathered.at[v, of], of, a_send.at[v, first + i], to)
            copy.start()
            started.append(copy)

    later = 4 + 2 * len(peers)

    def forward_x(v):
        forward(v, beside - c + 1, [peer + c for peer in peers], later)

    def forward_y(v):
        for i, peer in enumerate(peers):
            forward(v, peer, [beside], later + len(peers) + i)

    started = []
    a_start(1, beside_all, 1)
    a_start(1, peers_all, 4)
    weights[0].start()
    a_start(1, twin_all, 3)
    weights[4].start()
    weights[5].start()
    for v in range(2):
        gathered[v, s] = normed[2 * c + v]
    ring_step(0)

    zero_rows = jnp.zeros((COLS, 9 * 128), F32)
    taps[0:COLS, :] = zero_rows
    taps[COLS + places :, :] = zero_rows
    step = places // 2
    col = lax.rem(lax.broadcasted_iota(jnp.int32, (step, 128), 0), COLS)

    def convolve(v):
        rows = gathered[v].reshape(places, chans)
        taps[COLS : COLS + places, :] = dot_trans(rows, wsp[...].reshape(9 * 128, chans))
        for part_of in range(2):
            base = part_of * step

            def column(j):
                total = None
                for tap in range(3):
                    start = base + tap * COLS
                    lane = (tap * 3 + j) * 128
                    term = taps[start : start + step, lane : lane + 128]
                    total = term if total is None else total + term
                return total

            left = jnp.where(col == 0, 0.0, pltpu.roll(column(0), 1, 0))
            right = jnp.where(col == COLS - 1, 0.0, pltpu.roll(column(2), step - 1, 0))
            total = left + column(1) + right
            total = total * (1.0 / (1.0 + jnp.exp(-total)))
            act[v, base : base + step] = total.astype(BF16)

    a_start(0, beside_all, 1)
    a_start(0, peers_all, 4)
    a_start(0, twin_all, 3)
    for copy in weights[1:4]:
        copy.start()
    forward_x(1)
    forward_y(1)
    forward_x(0)
    forward_y(0)
    ring_step(1)
    loads[2].wait()
    weights[0].wait_recv()
    a_wait(1, twin)
    a_wait(1, beside - c)
    for peer in peers:
        a_wait(1, peer + 1)
    for peer in peers:
        for core in range(2):
            a_wait(1, peer + 2 - 4 * y + core)
    convolve(1)
    after = lax.rem(tau + 1, taus)
    edge_copy = send(
        act.at[1], edge, e_send.at[0], e_recv.at[0], after // 2, 2 * k + lax.rem(after, 2)
    )
    edge_copy.start()
    ring_step(2)
    loads[3].wait()
    weights[1].wait_recv()
    a_wait(0, twin)
    a_wait(0, beside - c)
    for peer in peers:
        a_wait(0, peer + 1)
    for peer in peers:
        for core in range(2):
            a_wait(0, peer + 2 - 4 * y + core)
    convolve(0)
    edge_copy.wait_recv()

    half_rows = spaces // 2
    near = s // half_rows

    def c_copy(half, side, d):
        to = side * half_rows + lax.rem(s + 3 * d, half_rows)
        return send(
            part.at[to, half],
            part_in.at[half, k, c],
            c_send.at[half, to],
            c_recv.at[half, s],
            o,
            to,
        )

    def c_from(half):
        def make(d):
            frm = lax.rem(s + d, spaces)
            return send(
                part.at[0, half],
                part_in.at[half, frm // 2, lax.rem(frm, 2)],
                c_send.at[half, d],
                c_recv.at[half, frm],
                o,
                frm,
            )

        return make

    sides = ((1 - near, 0), (near, 1))
    for side, first in sides:
        at = pl.ds(pl.multiple_of(side * step, step), step)
        pair = jnp.concatenate([act[0, at], act[1, at]], axis=1)
        total = dot_plain(pair, wtm[1:].reshape(256, chans))
        total = total + dot_plain(edge[at], wtm[0].reshape(128, chans))
        rows = pl.ds(side * half_rows, half_rows)
        part[rows] = total.reshape(half_rows, 2, 8, chans).astype(BF16)
        each(half_rows, functools.partial(c_copy, 0, side), lambda copy: copy.start(), first)
    for side, first in sides:
        each(half_rows, functools.partial(c_copy, 1, side), lambda copy: copy.start(), first)
        for half in range(2):
            sent.append((half_rows, functools.partial(c_copy, half, side), first))
    for half in range(2):
        part_in[half, k, c] = part[s, half]

    pass_on()
    weights[2].wait_recv()
    weights[3].wait_recv()
    loads[5].wait()
    loads[6].wait()
    for copy in passed:
        copy.wait_recv()
    ring_step(3)
    wqkv_turned[...] = wqkv[...].reshape(3 * 4 * HD, chans).T
    ring_step(4)
    loads[4].wait()
    upper = lax.broadcasted_iota(jnp.int32, (8, chans), 0) < 4

    def d_target(q, to_x):
        to_o, to_c = worker(x, c, q)
        return to_o, to_x * 4 + y * 2 + to_c

    def d_copy(q, to_x):
        to_o, to_s = d_target(q, to_x)
        i = q * xs + to_x
        return send(d_out.at[q], d_in.at[o], d_send.at[i], d_recv.at[o], to_o, to_s)

    def is_here(to_o, to_s):
        return jnp.logical_and(to_o == o, to_s == s)

    for half in range(2):
        each(spaces, c_from(half), lambda copy: copy.wait_recv(), 1)
        if half == 1:
            pass
        total = jnp.sum(part_in[half].astype(F32), axis=0)
        rounded = total.astype(BF16)
        down[half] = rounded
        wide = rms(rounded.astype(F32), again[...])
        first, second = wide[0], wide[1]
        d_out[2 * half] = jnp.where(upper, first, pltpu.roll(second, 4, 0)).astype(BF16)
        d_out[2 * half + 1] = jnp.where(upper, pltpu.roll(first, 4, 0), second).astype(BF16)
        for q in (2 * half, 2 * half + 1):
            for d in (2, 1, 3, 0):
                if d >= xs:
                    continue
                to_x = lax.rem(x + d, xs)
                here = is_here(*d_target(q, to_x))

                @pl.when(here)
                def _(q=q):
                    pltpu.make_async_copy(d_out.at[q], d_in.at[o], d_recv.at[o]).start()

                @pl.when(jnp.logical_not(here))
                def _(q=q, to_x=to_x):
                    d_copy(q, to_x).start()


    def d_from(i):
        return send(d_out.at[0], d_in.at[i], d_send.at[0], d_recv.at[i], i, served)

    each(orbits, d_from, lambda copy: copy.wait_recv())
    rows = d_in[...].astype(F32).reshape(pairs, chans).astype(BF16)
    qkv = dot_plain(rows, wqkv_turned[...])
    head_of = lax.broadcasted_iota(jnp.int32, (pairs, 4 * HD), 1) // HD
    query = qkv[:, : 4 * HD]
    key = qkv[:, 4 * HD : 8 * HD].astype(BF16)
    value = qkv[:, 8 * HD :].astype(BF16)
    apart = [jnp.where(head_of == head, query, 0.0).astype(BF16) for head in range(4)]
    scores = dot_trans(jnp.concatenate(apart, axis=0), key) * (HD**-0.5)
    left_place = lax.rem(lax.broadcasted_iota(jnp.int32, scores.shape, 0), QUARTERS)
    right_place = lax.rem(lax.broadcasted_iota(jnp.int32, scores.shape, 1), QUARTERS)
    scores = jnp.where(left_place == right_place, scores, -jnp.inf)
    grown = jnp.exp(scores - jnp.max(scores, axis=-1, keepdims=True))
    probs = (grown * (1.0 / jnp.sum(grown, axis=-1, keepdims=True))).astype(BF16)
    every = dot_plain(probs, value)
    mixed = every[:pairs]
    for head in range(1, 4):
        mixed = jnp.where(head_of == head, every[head * pairs : (head + 1) * pairs], mixed)
    projected = dot_plain(mixed.astype(BF16), wout[...].reshape(4 * HD, chans))
    proj[...] = projected.reshape(orbits, 8, chans).astype(BF16)

    def f_copy(i):
        return send(proj.at[i], f_in.at[x, wq], f_send.at[i], f_recv.at[4 * x + wq], i, served)

    def f_start(d, carry):
        i = lax.rem(d, 2) * (orbits // 2) + lax.rem(orbits // 2 * 4 + (1 - 2 * lax.rem(d // 2 + 1, 2)) * ((d // 2 + 1) // 2), orbits // 2)
        here = is_here(i, served)

        @pl.when(here)
        def _():
            pltpu.make_async_copy(proj.at[i], f_in.at[x, wq], f_recv.at[4 * x + wq]).start()

        @pl.when(jnp.logical_not(here))
        def _():
            f_copy(i).start()

        return carry

    lax.fori_loop(0, orbits, f_start, 0)

    def f_from(i):
        return send(
            proj.at[0], f_in.at[i // 4, lax.rem(i, 4)], f_send.at[0], f_recv.at[i], o, twin
        )

    for copy in weights + passed + started:
        copy.wait_send()
    edge_copy.wait_send()
    for count, make, first in sent:
        each(count, make, lambda copy: copy.wait_send(), first)

    for q in range(4):
        for to_x in range(xs):

            @pl.when(jnp.logical_not(is_here(*d_target(q, to_x))))
            def _(q=q, to_x=to_x):
                d_copy(q, to_x).wait_send()

    def f_drain(i, carry):
        @pl.when(jnp.logical_not(is_here(i, served)))
        def _():
            f_copy(i).wait_send()

        return carry

    lax.fori_loop(0, orbits, f_drain, 0)

    each(4 * xs, f_from, lambda copy: copy.wait_recv())
    for half in range(2):
        low = jnp.sum(f_in[:, 2 * half].astype(F32), axis=0)
        high = jnp.sum(f_in[:, 2 * half + 1].astype(F32), axis=0)
        first = jnp.where(upper, low, pltpu.roll(high, 4, 0))
        second = jnp.where(upper, pltpu.roll(low, 4, 0), high)
        for t, more in ((0, first), (1, second)):
            bottom = (down[half, t].astype(F32) + more).astype(BF16).astype(F32)
            at = slice(8 * half, 8 * half + 8)
            for view in (2 * t, 2 * t + 1):
                bot_ref[view, 0, at] = (lat[view, 0, at].astype(F32) + bottom).astype(BF16)


def body(latents, conv_gain, spatial_weight, temporal_weight, attn_gain, qkv_weight, out_weight):
    orbits, spaces = lax.axis_size("orbit"), lax.axis_size("space")
    chans = latents.shape[-1]
    chips, xs = spaces // 2, spaces // 4
    places = spaces * COLS
    vmem = pltpu.VMEM
    sem = pltpu.SemaphoreType.DMA
    return pl.pallas_call(
        functools.partial(level_kernel, orbits, spaces),
        out_shape=jax.ShapeDtypeStruct((4, 1, COLS, chans), BF16),
        in_specs=[pl.BlockSpec(memory_space=pltpu.HBM)] * 7,
        out_specs=pl.BlockSpec(memory_space=pltpu.VMEM),
        scratch_shapes=[
            vmem((4, 1, COLS, chans), BF16),
            vmem((1, chans), F32),
            vmem((1, chans), F32),
            vmem((9, 2, 64, chans), BF16),
            vmem((3, 2, 64, chans), BF16),
            vmem((3, 4, 64, chans), BF16),
            vmem((4, 64, chans), BF16),
            vmem((chans, 3 * 4 * HD), BF16),
            vmem((4, COLS, chans), BF16),
            vmem((2, spaces, COLS, chans), BF16),
            vmem((places + 2 * COLS, 9 * 128), F32),
            vmem((2, places, 128), BF16),
            vmem((places, 128), BF16),
            vmem((spaces, 2, 8, chans), BF16),
            vmem((2, chips, 2, 8, chans), BF16),
            vmem((2, 2, 8, chans), BF16),
            vmem((QUARTERS, 8, chans), BF16),
            vmem((orbits, 8, chans), BF16),
            vmem((orbits, 8, chans), BF16),
            vmem((xs, QUARTERS, 8, chans), BF16),
            sem((7,)),
            pltpu.SemaphoreType.REGULAR((4,)),
            sem((4,)),
            sem((4,)),
            sem((4,)),
            sem((4,)),
            sem((2, 4 + 2 * spaces)),
            sem((2, spaces)),
            sem((1,)),
            sem((1,)),
            sem((2, spaces)),
            sem((2, spaces)),
            sem((spaces,)),
            sem((orbits,)),
            sem((orbits,)),
            sem((spaces,)),
        ],
        compiler_params=pltpu.CompilerParams(
            collective_id=0, has_side_effects=True, vmem_limit_bytes=40 * 2**20
        ),
    )(
        *(
            pltpu.with_memory_space_constraint(array, pltpu.HBM)
            for array in (
                latents,
                conv_gain.reshape(1, chans),
                spatial_weight.reshape(9, 64, chans),
                temporal_weight,
                attn_gain.reshape(1, chans),
                qkv_weight,
                out_weight,
            )
        )
    )


def solution(mesh):
    return jax.shard_map(
        body,
        mesh=mesh,
        in_specs=(
            P("orbit", "space", None, None),
            P(),
            P(None, None, "space", None),
            P(None, "space", None),
            P(),
            P(None, "space", None),
            P("space", None),
        ),
        out_specs=P("orbit", "space", None, None),
        check_vma=False,
    )
```

```python
import functools

import jax
import jax.numpy as jnp
from jax import lax
from jax.experimental import pallas as pl
from jax.experimental.pallas import tpu as pltpu
from jax.sharding import PartitionSpec as P

HD = 64
COLS = 16
QUARTERS = 4
EPS = 1e-06
MESH = pl.DeviceIdType.MESH
F32 = jnp.float32
BF16 = jnp.bfloat16


def dot_trans(left, right):
    return lax.dot_general(left, right, (((1,), (1,)), ((), ())), preferred_element_type=F32)


def dot_plain(left, right):
    return jnp.dot(left, right, preferred_element_type=F32)


def rms(wide, gain):
    return wide * lax.rsqrt(jnp.mean(wide * wide, axis=-1, keepdims=True) + EPS) * gain


def level_kernel(
    orbits,
    spaces,
    lat_hbm,
    cgain_hbm,
    sw_hbm,
    tw_hbm,
    again_hbm,
    qw_hbm,
    ow_hbm,
    bot_ref,
    lat,
    cgain,
    again,
    wsp,
    wtm,
    wqkv,
    wout,
    wqkv_turned,
    apart_bias,
    normed,
    gathered,
    taps,
    act,
    edge,
    part,
    part_in,
    down,
    d_out,
    d_in,
    proj,
    f_in,
    local_sem,
    ring_sem,
    w_send,
    w_recv,
    y_send,
    y_recv,
    a_send,
    a_recv,
    e_send,
    e_recv,
    c_send,
    c_recv,
    d_send,
    d_recv,
    f_send,
    f_recv,
):
    xs = spaces // 4
    chips = spaces // 2
    taus = 2 * orbits
    chans = lat.shape[-1]
    places = spaces * COLS
    pairs = 8 * orbits
    o = lax.axis_index("orbit")
    s = lax.axis_index("space")
    c = lax.rem(s, 2)
    k = s // 2
    y = lax.rem(k, 2)
    x = s // 4
    slot = lax.rem(s, 4)
    tau = 2 * o + c
    twin = s + 1 - 2 * c
    beside = s + 2 - 4 * y
    across = lax.rem(o + orbits // 2, orbits)

    def worker(of_x, of_c, q):
        if xs == 1:
            return q, of_c
        return (of_x // 2) * 8 + of_c * 4 + q, lax.rem(of_x, 2)

    if xs == 1:
        wx, wc, wq = 0, c, o
    else:
        wx, wc, wq = (o // 8) * 2 + c, lax.rem(o, 8) // 4, lax.rem(o, 4)
    served = wx * 4 + y * 2 + wc

    def send(src, dst, ssem, rsem, to_o, to_s):
        return pltpu.make_async_remote_copy(
            src_ref=src,
            dst_ref=dst,
            send_sem=ssem,
            recv_sem=rsem,
            device_id=(to_o, to_s),
            device_id_type=MESH,
        )

    sent = []

    def each(count, make, what, first=0):
        def one(d, carry):
            what(make(d))
            return carry

        lax.fori_loop(first, count, one, 0)

    loads = [
        pltpu.make_async_copy(lat_hbm, lat, local_sem.at[0]),
        pltpu.make_async_copy(cgain_hbm, cgain, local_sem.at[1]),
        pltpu.make_async_copy(sw_hbm, wsp.at[:, c], local_sem.at[2]),
        pltpu.make_async_copy(tw_hbm, wtm.at[:, c], local_sem.at[3]),
        pltpu.make_async_copy(again_hbm, again, local_sem.at[4]),
        pltpu.make_async_copy(qw_hbm, wqkv.at[:, slot], local_sem.at[5]),
        pltpu.make_async_copy(ow_hbm, wout.at[slot], local_sem.at[6]),
    ]
    for load in loads:
        load.start()

    barrier = pltpu.get_barrier_semaphore()

    def signal(sem, to_o, to_s):
        pl.semaphore_signal(sem, inc=1, device_id=(to_o, to_s), device_id_type=MESH)

    peers = [lax.rem(x + d, xs) * 4 + 2 * y for d in (1, xs - 1, 2) if d < xs]
    peers = peers[: xs - 1]
    beside_all = [(beside - c + core, core) for core in range(2)]
    peers_all = [(peer + core, core) for peer in peers for core in range(2)]
    twin_all = [(twin, 1 - c)]
    for to, _ in peers_all + beside_all + twin_all:
        signal(barrier, o, to)
    signal(barrier, lax.rem(o + 1, orbits), s)
    signal(barrier, lax.rem(o + orbits - 1, orbits), s)
    signal(barrier, across, beside)

    rounds = []
    distance = 1
    while distance < orbits:
        rounds.append(distance)
        distance *= 2

    def round_signal(i):
        signal(ring_sem.at[i], lax.rem(o + rounds[i], orbits), s)
        if 2 * rounds[i] != orbits:
            signal(ring_sem.at[i], lax.rem(o + orbits - rounds[i], orbits), s)

    def round_wait(i):
        pl.semaphore_wait(ring_sem.at[i], 1 if 2 * rounds[i] == orbits else 2)

    def ring_step(i):
        if 0 < i <= len(rounds):
            round_wait(i - 1)
        if i < len(rounds):
            round_signal(i)

    loads[0].wait()
    loads[1].wait()
    row = rms(lat[...].astype(F32).reshape(4 * COLS, chans), cgain[...]).astype(BF16)
    normed[...] = row.reshape(4, COLS, chans)
    pl.semaphore_wait(barrier, 2 * len(peers) + 3 + 3)

    weights = [
        send(sw_hbm, wsp.at[:, c], w_send.at[0], w_recv.at[0], o, twin),
        send(tw_hbm, wtm.at[:, c], w_send.at[1], w_recv.at[1], o, twin),
        send(qw_hbm, wqkv.at[:, slot], w_send.at[2], w_recv.at[2], o, twin),
        send(ow_hbm, wout.at[slot], w_send.at[3], w_recv.at[3], o, twin),
    ]
    theirs = 2 - 2 * y + c
    weights.append(
        send(qw_hbm, wqkv.at[:, slot], y_send.at[0], y_recv.at[0], across, beside)
    )
    weights.append(
        send(ow_hbm, wout.at[slot], y_send.at[1], y_recv.at[1], across, beside)
    )
    passed = [
        send(wqkv.at[:, theirs], wqkv.at[:, theirs], y_send.at[2], y_recv.at[2], o, twin),
        send(wout.at[theirs], wout.at[theirs], y_send.at[3], y_recv.at[3], o, twin),
    ]

    def pass_on():
        weights[4].wait_recv()
        passed[0].start()
        weights[5].wait_recv()
        passed[1].start()

    def a_row(v, src, of, ssem, to):
        return send(src, gathered.at[v, of], ssem, a_recv.at[v, of], o, to)

    def a_wait(v, of):
        a_row(v, gathered.at[v, of], of, a_send.at[v, 0], twin).wait_recv()

    def a_own(v, to, core, i):
        return a_row(v, normed.at[2 * core + v], s, a_send.at[v, i], to)

    def a_start(v, targets, first):
        for i, (to, core) in enumerate(targets):
            copy = a_own(v, to, core, first + i)
            copy.start()
            started.append(copy)

    def forward(v, of, targets, first):
        a_wait(v, of)
        for i, to in enumerate(targets):
            copy = a_row(v, gathered.at[v, of], of, a_send.at[v, first + i], to)
            copy.start()
            started.append(copy)

    later = 4 + 2 * len(peers)

    def forward_x(v):
        forward(v, beside - c + 1, [peer + c for peer in peers], later)

    def forward_y(v):
        for i, peer in enumerate(peers):
            forward(v, peer, [beside], later + len(peers) + i)

    started = []
    a_start(1, beside_all, 1)
    a_start(1, peers_all, 4)
    weights[0].start()
    a_start(1, twin_all, 3)
    for v in range(2):
        gathered[v, s] = normed[2 * c + v]
    ring_step(0)

    zero_rows = jnp.zeros((COLS, 9 * 128), F32)
    taps[0:COLS, :] = zero_rows
    taps[COLS + places :, :] = zero_rows
    step = places // 2
    col = lax.rem(lax.broadcasted_iota(jnp.int32, (step, 128), 0), COLS)

    def convolve(v):
        rows = gathered[v].reshape(places, chans)
        taps[COLS : COLS + places, :] = dot_trans(rows, wsp[...].reshape(9 * 128, chans))
        for part_of in range(2):
            base = part_of * step

            def column(j):
                total = None
                for tap in range(3):
                    start = base + tap * COLS
                    lane = (tap * 3 + j) * 128
                    term = taps[start : start + step, lane : lane + 128]
                    total = term if total is None else total + term
                return total

            left = jnp.where(col == 0, 0.0, pltpu.roll(column(0), 1, 0))
            right = jnp.where(col == COLS - 1, 0.0, pltpu.roll(column(2), step - 1, 0))
            total = left + column(1) + right
            total = total * (1.0 / (1.0 + jnp.exp(-total)))
            act[v, base : base + step] = total.astype(BF16)

    a_start(0, beside_all, 1)
    a_start(0, peers_all, 4)
    a_start(0, twin_all, 3)
    for copy in weights[1:]:
        copy.start()
    forward_x(1)
    forward_y(1)
    forward_x(0)
    forward_y(0)
    ring_step(1)
    loads[2].wait()
    weights[0].wait_recv()
    a_wait(1, twin)
    a_wait(1, beside - c)
    for peer in peers:
        a_wait(1, peer + 1)
    for peer in peers:
        for core in range(2):
            a_wait(1, peer + 2 - 4 * y + core)
    convolve(1)
    after = lax.rem(tau + 1, taus)
    edge_copy = send(
        act.at[1], edge, e_send.at[0], e_recv.at[0], after // 2, 2 * k + lax.rem(after, 2)
    )
    edge_copy.start()
    ring_step(2)
    loads[3].wait()
    weights[1].wait_recv()
    a_wait(0, twin)
    a_wait(0, beside - c)
    for peer in peers:
        a_wait(0, peer + 1)
    for peer in peers:
        for core in range(2):
            a_wait(0, peer + 2 - 4 * y + core)
    convolve(0)
    edge_copy.wait_recv()

    half_rows = spaces // 2
    near = s // half_rows

    def c_copy(half, side, d):
        to = side * half_rows + lax.rem(s + 3 * d, half_rows)
        return send(
            part.at[to, half],
            part_in.at[half, k, c],
            c_send.at[half, to],
            c_recv.at[half, s],
            o,
            to,
        )

    def c_from(half):
        def make(d):
            frm = lax.rem(s + d, spaces)
            return send(
                part.at[0, half],
                part_in.at[half, frm // 2, lax.rem(frm, 2)],
                c_send.at[half, d],
                c_recv.at[half, frm],
                o,
                frm,
            )

        return make

    sides = ((1 - near, 0), (near, 1))
    for side, first in sides:
        at = pl.ds(pl.multiple_of(side * step, step), step)
        pair = jnp.concatenate([act[0, at], act[1, at]], axis=1)
        total = dot_plain(pair, wtm[1:].reshape(256, chans))
        total = total + dot_plain(edge[at], wtm[0].reshape(128, chans))
        rows = pl.ds(side * half_rows, half_rows)
        part[rows] = total.reshape(half_rows, 2, 8, chans).astype(BF16)
        each(half_rows, functools.partial(c_copy, 0, side), lambda copy: copy.start(), first)
    for side, first in sides:
        each(half_rows, functools.partial(c_copy, 1, side), lambda copy: copy.start(), first)
        for half in range(2):
            sent.append((half_rows, functools.partial(c_copy, half, side), first))
    for half in range(2):
        part_in[half, k, c] = part[s, half]

    pass_on()
    weights[2].wait_recv()
    weights[3].wait_recv()
    loads[5].wait()
    loads[6].wait()
    for copy in passed:
        copy.wait_recv()
    ring_step(3)
    wqkv_turned[...] = wqkv[...].reshape(3 * 4 * HD, chans).T
    ring_step(4)
    loads[4].wait()
    upper = lax.broadcasted_iota(jnp.int32, (8, chans), 0) < 4

    def d_target(q, to_x):
        to_o, to_c = worker(x, c, q)
        return to_o, to_x * 4 + y * 2 + to_c

    def d_copy(q, to_x):
        to_o, to_s = d_target(q, to_x)
        i = q * xs + to_x
        return send(d_out.at[q], d_in.at[o], d_send.at[i], d_recv.at[o], to_o, to_s)

    def is_here(to_o, to_s):
        return jnp.logical_and(to_o == o, to_s == s)

    for half in range(2):
        each(spaces, c_from(half), lambda copy: copy.wait_recv(), 1)
        if half == 1:
            pass
        total = jnp.sum(part_in[half].astype(F32), axis=0)
        rounded = total.astype(BF16)
        down[half] = rounded
        wide = rms(rounded.astype(F32), again[...])
        first, second = wide[0], wide[1]
        d_out[2 * half] = jnp.where(upper, first, pltpu.roll(second, 4, 0)).astype(BF16)
        d_out[2 * half + 1] = jnp.where(upper, pltpu.roll(first, 4, 0), second).astype(BF16)
        for q in (2 * half, 2 * half + 1):
            for d in (2, 1, 3, 0):
                if d >= xs:
                    continue
                to_x = lax.rem(x + d, xs)
                if d != 0:
                    d_copy(q, to_x).start()
                    continue
                here = is_here(*d_target(q, to_x))

                @pl.when(here)
                def _(q=q):
                    pltpu.make_async_copy(d_out.at[q], d_in.at[o], d_recv.at[o]).start()

                @pl.when(jnp.logical_not(here))
                def _(q=q, to_x=to_x):
                    d_copy(q, to_x).start()

    rows_of = (4 * pairs, pairs)
    left_place = lax.rem(lax.broadcasted_iota(jnp.int32, rows_of, 0), QUARTERS)
    right_place = lax.rem(lax.broadcasted_iota(jnp.int32, rows_of, 1), QUARTERS)
    apart_bias[...] = jnp.where(left_place == right_place, 0.0, -jnp.inf)

    def d_from(i):
        return send(d_out.at[0], d_in.at[i], d_send.at[0], d_recv.at[i], i, served)

    each(orbits, d_from, lambda copy: copy.wait_recv())
    rows = d_in[...].astype(F32).reshape(pairs, chans).astype(BF16)
    qkv = dot_plain(rows, wqkv_turned[...])
    head_of = lax.broadcasted_iota(jnp.int32, (pairs, 4 * HD), 1) // HD
    query = qkv[:, : 4 * HD] * (HD**-0.5)
    key = qkv[:, 4 * HD : 8 * HD].astype(BF16)
    value = qkv[:, 8 * HD :].astype(BF16)
    apart = [jnp.where(head_of == head, query, 0.0).astype(BF16) for head in range(4)]
    scores = dot_trans(jnp.concatenate(apart, axis=0), key) + apart_bias[...]
    grown = jnp.exp(scores - jnp.max(scores, axis=-1, keepdims=True))
    probs = (grown * (1.0 / jnp.sum(grown, axis=-1, keepdims=True))).astype(BF16)
    every = dot_plain(probs, value)
    mixed = every[:pairs]
    for head in range(1, 4):
        mixed = jnp.where(head_of == head, every[head * pairs : (head + 1) * pairs], mixed)
    projected = dot_plain(mixed.astype(BF16), wout[...].reshape(4 * HD, chans))
    proj[...] = projected.reshape(orbits, 8, chans).astype(BF16)

    def f_copy(i):
        return send(proj.at[i], f_in.at[x, wq], f_send.at[i], f_recv.at[4 * x + wq], i, served)

    def f_start(d, carry):
        i = lax.rem(d, 2) * (orbits // 2) + lax.rem(orbits // 2 * 4 + (1 - 2 * lax.rem(d // 2 + 1, 2)) * ((d // 2 + 1) // 2), orbits // 2)
        here = is_here(i, served)

        @pl.when(here)
        def _():
            pltpu.make_async_copy(proj.at[i], f_in.at[x, wq], f_recv.at[4 * x + wq]).start()

        @pl.when(jnp.logical_not(here))
        def _():
            f_copy(i).start()

        return carry

    lax.fori_loop(0, orbits, f_start, 0)

    def f_from(i):
        return send(
            proj.at[0], f_in.at[i // 4, lax.rem(i, 4)], f_send.at[0], f_recv.at[i], o, twin
        )

    for copy in weights + passed + started:
        copy.wait_send()
    edge_copy.wait_send()
    for count, make, first in sent:
        each(count, make, lambda copy: copy.wait_send(), first)

    for q in range(4):
        for to_x in range(xs):

            @pl.when(jnp.logical_not(is_here(*d_target(q, to_x))))
            def _(q=q, to_x=to_x):
                d_copy(q, to_x).wait_send()

    def f_drain(i, carry):
        @pl.when(jnp.logical_not(is_here(i, served)))
        def _():
            f_copy(i).wait_send()

        return carry

    lax.fori_loop(0, orbits, f_drain, 0)

    each(4 * xs, f_from, lambda copy: copy.wait_recv())
    for half in range(2):
        low = jnp.sum(f_in[:, 2 * half].astype(F32), axis=0)
        high = jnp.sum(f_in[:, 2 * half + 1].astype(F32), axis=0)
        first = jnp.where(upper, low, pltpu.roll(high, 4, 0))
        second = jnp.where(upper, pltpu.roll(low, 4, 0), high)
        bot_ref[0, half] = (down[half, 0].astype(F32) + first).astype(BF16)
        bot_ref[1, half] = (down[half, 1].astype(F32) + second).astype(BF16)


def body(latents, conv_gain, spatial_weight, temporal_weight, attn_gain, qkv_weight, out_weight):
    orbits, spaces = lax.axis_size("orbit"), lax.axis_size("space")
    chans = latents.shape[-1]
    chips, xs = spaces // 2, spaces // 4
    places = spaces * COLS
    vmem = pltpu.VMEM
    sem = pltpu.SemaphoreType.DMA
    bottom = pl.pallas_call(
        functools.partial(level_kernel, orbits, spaces),
        out_shape=jax.ShapeDtypeStruct((2, 2, 8, chans), BF16),
        in_specs=[pl.BlockSpec(memory_space=pltpu.HBM)] * 7,
        out_specs=pl.BlockSpec(memory_space=pltpu.VMEM),
        scratch_shapes=[
            vmem((4, 1, COLS, chans), BF16),
            vmem((1, chans), F32),
            vmem((1, chans), F32),
            vmem((9, 2, 64, chans), BF16),
            vmem((3, 2, 64, chans), BF16),
            vmem((3, 4, 64, chans), BF16),
            vmem((4, 64, chans), BF16),
            vmem((chans, 3 * 4 * HD), BF16),
            vmem((32 * orbits, 8 * orbits), F32),
            vmem((4, COLS, chans), BF16),
            vmem((2, spaces, COLS, chans), BF16),
            vmem((places + 2 * COLS, 9 * 128), F32),
            vmem((2, places, 128), BF16),
            vmem((places, 128), BF16),
            vmem((spaces, 2, 8, chans), BF16),
            vmem((2, chips, 2, 8, chans), BF16),
            vmem((2, 2, 8, chans), BF16),
            vmem((QUARTERS, 8, chans), BF16),
            vmem((orbits, 8, chans), BF16),
            vmem((orbits, 8, chans), BF16),
            vmem((xs, QUARTERS, 8, chans), BF16),
            sem((7,)),
            pltpu.SemaphoreType.REGULAR((4,)),
            sem((4,)),
            sem((4,)),
            sem((4,)),
            sem((4,)),
            sem((2, 4 + 2 * spaces)),
            sem((2, spaces)),
            sem((1,)),
            sem((1,)),
            sem((2, spaces)),
            sem((2, spaces)),
            sem((spaces,)),
            sem((orbits,)),
            sem((orbits,)),
            sem((spaces,)),
        ],
        compiler_params=pltpu.CompilerParams(
            collective_id=0, has_side_effects=True, vmem_limit_bytes=40 * 2**20
        ),
    )(
        *(
            pltpu.with_memory_space_constraint(array, pltpu.HBM)
            for array in (
                latents,
                conv_gain.reshape(1, chans),
                spatial_weight.reshape(9, 64, chans),
                temporal_weight,
                attn_gain.reshape(1, chans),
                qkv_weight,
                out_weight,
            )
        )
    )
    grown = jnp.repeat(bottom.reshape(2, COLS, chans), 2, axis=0)[:, None]
    return (latents.astype(F32) + grown.astype(F32)).astype(BF16)


def solution(mesh):
    return jax.shard_map(
        body,
        mesh=mesh,
        in_specs=(
            P("orbit", "space", None, None),
            P(),
            P(None, None, "space", None),
            P(None, "space", None),
            P(),
            P(None, "space", None),
            P("space", None),
        ),
        out_specs=P("orbit", "space", None, None),
        check_vma=False,
    )
```
